32 devices in a mesh: grp: 2 (over core), zon: 8 (over z, y), mer: 2 (over x).
Axes of the slice: x: 2, y: 2, z: 4, core: 2. Of those that a mesh axis runs over, the one named last changes fastest.
Arguments:
- model_state: float32 [4, 6, 128, 1024], P(None, 'grp', 'mer', 'zon'), may hold values from -4 to 4
- control: float32 [4, 6, 128, 1024], P('grp', None, 'mer', 'zon'), may hold values from -6 to 6
- error_std: float32 [4, 6, 128, 1024], P('grp', None, 'mer', 'zon'), may hold values from 0.3 to 3
- bottom_level: int32 [128, 1024], P('mer', 'zon'), may hold values from 0 to 6
- obs_count: int32 [2, 2, 8], P('grp', 'mer', 'zon'), may hold values from 1 to 256, as said below
- obs_corner: int32 [2, 2, 8, 256], P('grp', 'mer', 'zon'), may hold values from 0 to 98174, as said below
- obs_weight: float32 [2, 2, 8, 4, 256], P('grp', 'mer', 'zon'), may hold values from 0 to 1, as said below
- obs_value: float32 [2, 2, 8, 256], P('grp', 'mer', 'zon'), may hold values from -5 to 5
- obs_precision: float32 [2, 2, 8, 256], P('grp', 'mer', 'zon'), may hold values from 0.25 to 4
Outputs:
- gradient: float32 [4, 6, 128, 1024], P('grp', None, 'mer', 'zon')
The draws below stay inside these ranges and needn't reach their ends.
Inputs may be any that keep to these rules, and one draw needn't show every extreme that they name: `obs_count`: at least one live observation in every block, exactly 256 in some block. `obs_corner`: each slot's four interpolation cells lie in its own tile; padded slots also hold valid indices. `obs_weight`: the four weights of a slot are nonnegative and sum to one.
All inputs are finite; a program needn't handle non-finite values.
Results may differ from the reference program's by a relative error of at most 0.0003.
Values may be sent and summed in bfloat16 or wider, within the bound.
A program may use at most 64 MiB of HBM per device.

```python
import math
import jax
import jax.numpy as jnp
from jax import lax

FIELDS = 4
CX = 128
CY = 64
LEV = 6
CAP = 256
SWEEPS = 10
NX = 1024
NY = 128
N_GRP = 2
N_ZON = 8
N_MER = 2


def draw_obs_count(key, part):
    blocks = N_GRP * N_MER * N_ZON
    first_key, secondary_key = jax.random.split(key)
    counts = jax.random.randint(first_key, (blocks,), 1, CAP + 1)
    chosen = jax.random.randint(secondary_key, (), 0, blocks)
    counts = jnp.where(jnp.arange(blocks) == chosen, CAP, counts)
    return counts.reshape(N_GRP, N_MER, N_ZON).astype(jnp.int32)


def draw_obs_corner(key, part):
    keys = jax.random.split(key, 5)
    full_shape = (N_GRP, N_MER, N_ZON, CAP)
    field_pick = jax.random.randint(keys[0], full_shape, 0, 2)
    level_pick = jax.random.randint(keys[1], full_shape, 0, LEV)
    row_pick = jax.random.randint(keys[2], full_shape, 0, CY - 1)
    column = jax.random.randint(keys[3], full_shape, 0, CX - 1)
    corner = ((field_pick * LEV + level_pick) * CY + row_pick) * CX + column
    flattened = corner.reshape(-1)
    slots = flattened.shape[0]
    high_pos = jax.random.randint(keys[4], (), 0, slots)
    low_pos = (high_pos + 1) % slots
    positions = jnp.arange(slots)
    flattened = jnp.where(positions == high_pos, 2 * LEV * CY * CX - CX - 2, flattened)
    flattened = jnp.where(positions == low_pos, 0, flattened)
    return flattened.reshape(full_shape).astype(jnp.int32)


def draw_obs_weight(key, part):
    first_key, secondary_key = jax.random.split(key)
    full_shape = (N_GRP, N_MER, N_ZON, CAP)
    frac_x = jax.random.uniform(first_key, full_shape, jnp.float32)
    frac_y = jax.random.uniform(secondary_key, full_shape, jnp.float32)
    weights = jnp.stack([(1.0 - frac_x) * (1.0 - frac_y), frac_x * (1.0 - frac_y), (1.0 - frac_x) * frac_y, frac_x * frac_y], axis=3)
    return weights.astype(jnp.float32)


def place_ends(result, own_key, low, top_value):
    index_at = [jax.random.randint(jax.random.fold_in(own_key, axis), (), 0, length) for axis, length in enumerate(result.shape)]
    widest = result.shape.index(max(result.shape))
    beside = index_at[:widest] + [(index_at[widest] + 1) % result.shape[widest]] + index_at[widest + 1:]
    return result.at[tuple(index_at)].set(low).at[tuple(beside)].set(top_value)


def block_scale(own_key, extent, cuts, low, high):
    def one(dim, parts):
        steps = jax.random.uniform(jax.random.fold_in(jax.random.fold_in(own_key, 6), dim), (parts,), jnp.float32, low / len(cuts), high / len(cuts))
        return jnp.repeat(jnp.exp(steps), extent[dim] // parts).reshape((-1,) + (1,) * (len(extent) - dim - 1))

    gain = one(*cuts[0])
    for cut in cuts[1:]:
        gain = gain * one(*cut)
    return gain


def gaussian(own_key, extent, spread, limit, cuts=(), kind=jnp.bfloat16):
    values = jax.random.normal(own_key, extent, jnp.float32) * spread
    if len(cuts) > 0:
        values = block_scale(own_key, extent, cuts, -0.22, 0.18) * values
    return jnp.clip(values, min=-limit, max=limit).astype(kind)


def setup_inputs(seed: int = 0) -> dict:
    key_of = jax.random.split(jax.random.key(seed), 10)
    return {
        "model_state": gaussian(key_of[0], (FIELDS, LEV, NY, NX), 1.0, 4.0, ((1, 2), (2, 2), (3, 8)), jnp.float32),
        "control": gaussian(key_of[1], (FIELDS, LEV, NY, NX), 1.0, 6.0, ((0, 2), (2, 2), (3, 8)), jnp.float32),
        "error_std": jnp.clip(jnp.exp(math.log(3.0) - 2.3025851 * jax.random.uniform(key_of[2], (FIELDS, LEV, NY, NX), jnp.float32) ** block_scale(key_of[2], (FIELDS, LEV, NY, NX), ((0, 2), (2, 2), (3, 8)), -0.2, 0.2)), 0.3, 3.0),
        "bottom_level": place_ends(jax.random.randint(key_of[3], (NY, NX), 0, LEV + 1), jax.random.fold_in(key_of[3], 1), 0, LEV).astype(jnp.int32),
        "obs_count": draw_obs_count(jax.random.fold_in(key_of[9], 71), 0),
        "obs_corner": draw_obs_corner(jax.random.fold_in(key_of[9], 71), 0),
        "obs_weight": draw_obs_weight(jax.random.fold_in(key_of[9], 71), 0),
        "obs_value": gaussian(key_of[7], (N_GRP, N_MER, N_ZON, CAP), 1.0, 5.0, ((0, 2), (1, 2), (2, 8)), jnp.float32),
        "obs_precision": jnp.clip(jnp.exp(math.log(4.0) - 2.7725887 * jax.random.uniform(key_of[8], (N_GRP, N_MER, N_ZON, CAP), jnp.float32) ** block_scale(key_of[8], (N_GRP, N_MER, N_ZON, CAP), ((0, 2), (1, 2), (2, 8)), -0.2, 0.2)), 0.25, 4.0),
    }


SMOOTHING = 0.2
ADVECTION = 0.1
MIXING = 0.15


def extend(field_now, width):
    wrapped = jnp.concatenate([field_now[..., -width:], field_now, field_now[..., :width]], axis=-1)
    padding = [(0, 0)] * (field_now.ndim - 2) + [(width, width), (0, 0)]
    return jnp.pad(wrapped, padding)


def flux_sum(padded, mask_pad):
    centre = padded[..., 1:-1, 1:-1]
    summed = mask_pad[..., 1:-1, 2:] * (padded[..., 1:-1, 2:] - centre)
    summed = summed + mask_pad[..., 1:-1, :-2] * (padded[..., 1:-1, :-2] - centre)
    summed = summed + mask_pad[..., 2:, 1:-1] * (padded[..., 2:, 1:-1] - centre)
    summed = summed + mask_pad[..., :-2, 1:-1] * (padded[..., :-2, 1:-1] - centre)
    return mask_pad[..., 1:-1, 1:-1] * summed


def one_sweep(padded, mask_pad):
    return padded[..., 1:-1, 1:-1] + SMOOTHING * flux_sum(padded, mask_pad)


def reference(model_state, control, error_std, bottom_level, obs_count, obs_corner, obs_weight, obs_value, obs_precision):
    wet_mask = (lax.iota(jnp.int32, LEV)[:, None, None] < bottom_level[None]).astype(jnp.float32)
    mask_one = extend(wet_mask, 1)

    def advance(pieces):
        level_state, depth_level_mask = pieces
        padded = extend(level_state, 1)
        masked = padded * depth_level_mask
        centre = padded[:, 1:-1, 1:-1]
        grad_x = 0.5 * (masked[:, 1:-1, 2:] - masked[:, 1:-1, :-2])
        grad_y = 0.5 * (masked[:, 2:, 1:-1] - masked[:, :-2, 1:-1])
        shifted_values = centre - ADVECTION * (centre[2] * grad_x + centre[3] * grad_y) + MIXING * flux_sum(padded, depth_level_mask)
        return depth_level_mask[1:-1, 1:-1] * shifted_values

    prior_estimate = jnp.moveaxis(lax.map(advance, (jnp.moveaxis(model_state, 1, 0), mask_one)), 0, 1)

    def smooth(field_stack):
        def one_field(field_now):
            return lax.fori_loop(0, SWEEPS, lambda sweep_index, current: one_sweep(extend(current, 1), mask_one), field_now)
        return lax.map(one_field, field_stack)

    pair_index = lax.iota(jnp.int32, N_GRP)[:, None, None, None]
    mer_row = lax.iota(jnp.int32, N_MER)[None, :, None, None]
    zon_col = lax.iota(jnp.int32, N_ZON)[None, None, :, None]
    column = obs_corner % CX
    remainder = obs_corner // CX
    row_pick = remainder % CY
    remainder = remainder // CY
    level_pick = remainder % LEV
    field_pick = remainder // LEV
    global_index = (((2 * pair_index + field_pick) * LEV + level_pick) * NY + mer_row * CY + row_pick) * NX + zon_col * CX + column
    offsets = jnp.array([0, 1, NX, NX + 1], jnp.int32)
    corners = (global_index[..., None, :] + offsets[:, None]).astype(jnp.int32)
    live_slot = (lax.iota(jnp.int32, CAP) < obs_count[..., None]).astype(jnp.float32)

    def observe(field_stack):
        return jnp.sum(obs_weight * field_stack.reshape(-1)[corners], axis=3)

    innovation = live_slot * (obs_value - observe(prior_estimate))
    increment = wet_mask * error_std * smooth(control)
    misfit = live_slot * obs_precision * (observe(increment) - innovation)
    adjoint_obs = jnp.zeros((FIELDS * LEV * NY * NX,), jnp.float32).at[corners.reshape(-1)].add((obs_weight * misfit[..., None, :]).reshape(-1))
    adjoint_obs = adjoint_obs.reshape(control.shape)
    return control + smooth(wet_mask * error_std * adjoint_obs)
```

```python
import functools

import jax
import jax.numpy as jnp
from jax import lax
from jax.experimental import pallas as pl
from jax.experimental.pallas import tpu as pltpu
from jax.sharding import PartitionSpec as P

SWEEPS = 10
SMOOTHING = 0.2
ADVECTION = 0.1
MIXING = 0.15

MESH = pl.DeviceIdType.MESH
PAD = 16
ZONAL = [(1, 0), (-1, 0)]
MERIDIONAL = [(0, 1), (0, -1)]
SIDES = ZONAL + MERIDIONAL
DIRS = [(1, 1), (1, -1), (-1, 1), (-1, -1)] + ZONAL + MERIDIONAL


def pieces(value):
    parts = []
    for _ in range(2):
        part = value.astype(jnp.bfloat16)
        parts.append(part)
        value = value - part.astype(jnp.float32)
    return parts


def kernel(
    sizes,
    state_hbm,
    control_hbm,
    std_hbm,
    bottom_hbm,
    count_hbm,
    corner_hbm,
    weight_hbm,
    value_hbm,
    precision_hbm,
    out_ref,
    bottom_ref,
    count_ref,
    corner_ref,
    weight_ref,
    value_ref,
    precision_ref,
    state,
    state_rows,
    state_rows_in,
    state_cols,
    state_cols_in,
    back,
    back_in,
    field,
    turned_in,
    strips_out,
    strips,
    field_two,
    strips_out_two,
    strips_two,
    fold_ref,
    turned_out,
    depth_ref,
    ping,
    pong,
    bottom,
    bottom_side,
    keep_ref,
    gain_ref,
    std,
    smooth_ref,
    x_ref,
    rows_hot,
    rows_hot_t,
    obs_stack,
    corner_hot,
    local_sem,
    bot_send,
    bot_recv,
    st_send,
    st_recv,
    one_send,
    one_recv,
    two_send,
    two_recv,
    bg_send,
    bg_recv,
):
    n_zon, n_mer, levels, half, pair, fields, R, C = sizes
    w = SWEEPS
    planes = pair * levels
    tiles = (R + 2 * w + 7) // 8
    base = PAD - (8 * tiles - R) // 2
    columns = (C + 2 * w + 7) // 8
    column_base = PAD - (8 * columns - C) // 2
    g = lax.axis_index("grp")
    z = lax.axis_index("zon")
    m = lax.axis_index("mer")
    has = {-1: m > 0, 1: m < n_mer - 1}

    def device(dz, dm):
        return (g, lax.rem(z + dz + n_zon, n_zon), m + dm)

    def when(dm, action):
        if dm == 0:
            action()
        else:
            pl.when(has[dm])(action)

    barrier = pltpu.get_barrier_semaphore()
    pl.semaphore_signal(barrier, inc=1, device_id=(1 - g, z, m), device_id_type=MESH)
    for dz, dm in DIRS:
        def greet(dz=dz, dm=dm):
            pl.semaphore_signal(barrier, inc=1, device_id=device(dz, dm), device_id_type=MESH)
        when(dm, greet)

    load_control = pltpu.make_async_copy(control_hbm, field.at[:, pl.ds(PAD, R)], local_sem.at[0])
    load_state = pltpu.make_async_copy(state_hbm, state.at[:, pl.ds(8, R)], local_sem.at[1])
    load_std = pltpu.make_async_copy(std_hbm, std, local_sem.at[2])
    load_bottom = pltpu.make_async_copy(bottom_hbm, bottom_ref, local_sem.at[3])
    tables = [
        pltpu.make_async_copy(source, target, local_sem.at[4 + i])
        for i, (source, target) in enumerate([
            (count_hbm, count_ref),
            (corner_hbm, corner_ref),
            (weight_hbm, weight_ref),
            (value_hbm, value_ref),
            (precision_hbm, precision_ref),
        ])
    ]
    load_bottom.start()
    load_state.start()
    load_control.start()
    load_std.start()
    for table in tables:
        table.start()

    lane_r = lax.broadcasted_iota(jnp.int32, (R, C), 1)
    lane = lax.broadcasted_iota(jnp.int32, (8, C), 1)
    lane_pad = lax.broadcasted_iota(jnp.int32, (PAD, C), 1)

    def pack(source, target):
        def one(p, carry):
            first, last = carry
            u = source[p, pl.ds(PAD, R), :]
            here = (lane_r >= p * w) & (lane_r < p * w + w)
            last = jnp.where(here, pltpu.roll(u, lax.rem(p * w + w, C), axis=1), last)
            first = jnp.where(here, pltpu.roll(u, lax.rem(p * w, C), axis=1), first)
            return first, last
        zero = jnp.zeros((R, C), jnp.float32)
        first, last = lax.fori_loop(0, planes, one, (zero, zero))
        target[0] = last
        target[1] = first

    def span(dm):
        if dm == 0:
            return pl.ds(0, R), pl.ds(PAD, R)
        if dm == 1:
            return pl.ds(R - PAD, PAD), pl.ds(0, PAD)
        return pl.ds(0, PAD), pl.ds(PAD + R, PAD)

    def side(dz):
        return 0 if dz == 1 else 1

    def bottom_copy(i):
        dz, dm = DIRS[i]
        src, dst = span(dm)
        target = bottom.at[dst] if dz == 0 else bottom_side.at[side(dz), dst]
        return pltpu.make_async_remote_copy(
            src_ref=bottom_ref.at[src], dst_ref=target,
            send_sem=bot_send.at[i], recv_sem=bot_recv.at[i],
            device_id=device(dz, dm), device_id_type=MESH)

    def halo_copy(i, whole, packed, landed, send, recv):
        dz, dm = DIRS[i]
        src, dst = span(dm)
        if dz == 0:
            inner = pl.ds(PAD + R - w, w) if dm == 1 else pl.ds(PAD, w)
            outer = pl.ds(PAD - w, w) if dm == 1 else pl.ds(PAD + R, w)
            source, target = whole.at[:, inner], whole.at[:, outer]
        else:
            source, target = packed.at[side(dz), src], landed.at[side(dz), dst]
        return pltpu.make_async_remote_copy(
            src_ref=source, dst_ref=target, send_sem=send.at[i], recv_sem=recv.at[i],
            device_id=device(dz, dm), device_id_type=MESH)

    def one_copy(i):
        return halo_copy(i, field, strips_out, strips, one_send, one_recv)

    def two_copy(i):
        return halo_copy(i, field_two, strips_out_two, strips_two, two_send, two_recv)

    def state_copy(i):
        dz, dm = SIDES[i]
        if dz == 0:
            k = 0 if dm == 1 else 1
            source, target = state_rows.at[k], state_rows_in.at[k]
        else:
            source, target = state_cols.at[side(dz)], state_cols_in.at[side(dz)]
        return pltpu.make_async_remote_copy(
            src_ref=source, dst_ref=target, send_sem=st_send.at[i], recv_sem=st_recv.at[i],
            device_id=device(dz, dm), device_id_type=MESH)

    def start_all(copies, make):
        for i, (dz, dm) in enumerate(copies):
            when(dm, lambda i=i: make(i).start())

    def land_all(copies, make):
        for i, (dz, dm) in enumerate(copies):
            when(-dm, lambda i=i: make(i).wait_recv())

    def sent_all(copies, make):
        for i, (dz, dm) in enumerate(copies):
            when(dm, lambda i=i: make(i).wait_send())

    load_bottom.wait()
    bottom[pl.ds(PAD, R)] = bottom_ref[...]
    for dm, rows in ((-1, pl.ds(0, PAD)), (1, pl.ds(PAD + R, PAD))):
        def dry(rows=rows):
            empty = jnp.zeros((PAD, C), jnp.int32)
            bottom[rows] = empty
            bottom_side[0, rows] = empty
            bottom_side[1, rows] = empty
        pl.when(jnp.logical_not(has[dm]))(dry)

    load_state.wait()
    first = jnp.zeros((R, C), jnp.float32)
    last = jnp.zeros((R, C), jnp.float32)
    for q in range(fields * half):
        u = state[q, pl.ds(8, R), :]
        last = jnp.where(lane_r == q, pltpu.roll(u, (q + 1) % C, axis=1), last)
        first = jnp.where(lane_r == q, pltpu.roll(u, q, axis=1), first)
        state_rows[0, pl.ds(q, 1), :] = state[q, pl.ds(8 + R - 1, 1), :]
        state_rows[1, pl.ds(q, 1), :] = state[q, pl.ds(8, 1), :]
    state_cols[0] = last
    state_cols[1] = first

    edges = jnp.where(has[-1], 1, 0) + jnp.where(has[1], 1, 0)
    load_control.wait()
    pack(field, strips_out)
    pl.semaphore_wait(barrier, 3 + 3 * edges)
    start_all(DIRS, bottom_copy)
    start_all(SIDES, state_copy)
    start_all(DIRS, one_copy)

    for table in tables:
        table.wait()
    shift = C.bit_length() - 1
    slots = corner_ref.shape[1]
    corner = corner_ref[...]
    flat_row = lax.shift_right_logical(corner, jnp.full_like(corner, shift))
    column = corner - flat_row * C
    live = (lax.broadcasted_iota(jnp.int32, (1, slots), 1) < count_ref[...]).astype(jnp.float32)
    obs_stack[...] = jnp.zeros_like(obs_stack)
    obs_stack[pl.ds(0, 1), :] = column.astype(jnp.float32)
    obs_stack[pl.ds(1, 1), :] = flat_row.astype(jnp.float32)
    obs_stack[pl.ds(2, 4), :] = weight_ref[...]
    obs_stack[pl.ds(6, 1), :] = live * precision_ref[...]
    obs_stack[pl.ds(7, 1), :] = value_ref[...]
    turned = jnp.transpose(obs_stack[...])
    col_i = turned[:, 0:1].astype(jnp.int32)
    col_row = turned[:, 1:2].astype(jnp.int32)
    lane_s = lax.broadcasted_iota(jnp.int32, (slots, C), 1)
    here = lane_s == col_i
    beside = lane_s == col_i + 1
    for k in range(2):
        corner_hot[:, k * C:(k + 1) * C] = jnp.where(
            here, turned[:, 2 + 2 * k:3 + 2 * k], 0.0
        ) + jnp.where(beside, turned[:, 3 + 2 * k:4 + 2 * k], 0.0)
    scale = turned[:, 6:7]
    seen = turned[:, 7:8]
    for k in range(planes * R // C):
        ids = lax.broadcasted_iota(jnp.int32, (slots, C), 1) + k * C
        rows_hot[:, k * C:(k + 1) * C] = jnp.where(ids == col_row, 1.0, 0.0).astype(jnp.bfloat16)
        ids = lax.broadcasted_iota(jnp.int32, (C, slots), 0) + k * C
        rows_hot_t[k * C:(k + 1) * C, :] = jnp.where(ids == flat_row, 1.0, 0.0).astype(jnp.bfloat16)

    def strided(t):
        return pl.ds(base + t, 8, tiles)

    def strided_column(k):
        return pl.ds(column_base + k, 8, columns)

    spare = jnp.zeros((C - 8 * planes, C), jnp.float32)

    def turn(source, target):
        for t in range(tiles):
            rows = [source[p, strided(t), :] for p in range(planes)]
            target[t, pl.ds(PAD, C), :] = jnp.transpose(jnp.concatenate(rows + [spare], axis=0))

    def turn_back(target):
        for t in range(tiles):
            rows = jnp.transpose(turned_out[t, pl.ds(PAD, C), :])
            for p in range(planes):
                target[p, strided(t), :] = rows[8 * p:8 * p + 8]

    def unfold(landed, target):
        group = lax.shift_right_logical(lane_pad, jnp.full_like(lane_pad, 3))
        for h in range(2):
            rows = [landed[h, strided(t), :] for t in range(tiles)]
            rows.append(jnp.zeros((C - 8 * tiles, C), jnp.float32))
            fold_ref[h, pl.ds(8, C), :] = jnp.transpose(jnp.concatenate(rows, axis=0))
            offset = 8 if h else 8 + w - PAD
            moved = [
                pltpu.roll(fold_ref[h, pl.ds(offset + p * w, PAD), :], 8 * p, axis=1)
                for p in range(planes)
            ]
            for t in range(tiles):
                block = moved[0]
                for p in range(1, planes):
                    block = jnp.where(group == (t + p) % (C // 8), moved[p], block)
                target[t, pl.ds((PAD + C) * h, PAD), :] = pltpu.roll(block, (C - 8 * t) % C, axis=1)

    def arrive(whole, make, landed):
        for i, (dz, dm) in enumerate(DIRS):
            if dz == 0:
                when(-dm, lambda i=i: make(i).wait_recv())
        turn(whole, turned_in)
        for i, (dz, dm) in enumerate(DIRS):
            if dz != 0:
                when(-dm, lambda i=i: make(i).wait_recv())
        unfold(landed, turned_in)

    land_all(DIRS, bottom_copy)
    land_all(SIDES, state_copy)
    for k, dm, row in ((0, -1, 7), (1, 1, 8 + R)):
        def edge_in(k=k, row=row):
            for q in range(fields * half):
                state[q, pl.ds(row, 1), :] = state_rows_in[k, pl.ds(q, 1), :]
        def edge_none(row=row):
            for q in range(fields * half):
                state[q, pl.ds(row, 1), :] = jnp.zeros((1, C), jnp.float32)
        pl.when(has[dm])(edge_in)
        pl.when(jnp.logical_not(has[dm]))(edge_none)

    def neighbours(tile, before, after):
        east = jnp.where(lane_r == C - 1, after, pltpu.roll(tile, C - 1, axis=1))
        west = jnp.where(lane_r == 0, before, pltpu.roll(tile, 1, axis=1))
        return east, west

    deep = bottom[pl.ds(PAD, R), :]
    east_bottom, west_bottom = neighbours(
        deep,
        pltpu.roll(bottom_side[0, pl.ds(PAD, R), :], 1, axis=1),
        pltpu.roll(bottom_side[1, pl.ds(PAD, R), :], C - 1, axis=1),
    )

    def step_level(j, carry):
        level = g * half + j
        wet_c = (deep > level).astype(jnp.float32)
        wet_e = (east_bottom > level).astype(jnp.float32)
        wet_w = (west_bottom > level).astype(jnp.float32)
        wet_n = (bottom[pl.ds(PAD + 1, R), :] > level).astype(jnp.float32)
        wet_s = (bottom[pl.ds(PAD - 1, R), :] > level).astype(jnp.float32)
        vel_x = state[2 * half + j, pl.ds(8, R), :]
        vel_y = state[3 * half + j, pl.ds(8, R), :]
        for f in range(fields):
            q = f * half + j
            centre = state[q, pl.ds(8, R), :]
            east, west = neighbours(
                centre,
                pltpu.roll(state_cols_in[0], lax.rem(C - q, C), axis=1),
                pltpu.roll(state_cols_in[1], C - 1 - q, axis=1),
            )
            north = state[q, pl.ds(9, R), :]
            south = state[q, pl.ds(7, R), :]
            grad_x = 0.5 * (wet_e * east - wet_w * west)
            grad_y = 0.5 * (wet_n * north - wet_s * south)
            flux = wet_c * (
                wet_e * (east - centre) + wet_w * (west - centre)
                + wet_n * (north - centre) + wet_s * (south - centre)
            )
            back[q] = wet_c * (
                centre - ADVECTION * (vel_x * grad_x + vel_y * grad_y) + MIXING * flux
            )
        return carry

    lax.fori_loop(0, half, step_level, 0)
    share = pair * half
    give = pltpu.make_async_remote_copy(
        src_ref=back.at[pl.ds((1 - g) * share, share)], dst_ref=back_in,
        send_sem=bg_send, recv_sem=bg_recv, device_id=(1 - g, z, m), device_id_type=MESH)
    give.start()

    def stencil(source, emit):
        def column(k):
            return [source[t, k] for t in range(tiles)]

        first = column(0)
        before = [pltpu.roll(v, 1, axis=0) for v in column(columns - 1)]
        here = first
        for k in range(columns):
            if k < columns - 1:
                after = column(k + 1)
            else:
                after = [pltpu.roll(v, 7, axis=0) for v in first]
            south = pltpu.roll(here[tiles - 1], 1, axis=1)
            north = pltpu.roll(here[0], C - 1, axis=1)
            for t in range(tiles):
                below = here[t - 1] if t else south
                above = here[t + 1] if t < tiles - 1 else north
                emit(t, k, here[t], (before[t] + after[t]) + (below + above))
            before, here = here, after

    def depth_of(parts):
        stacked = jnp.concatenate(
            parts + [jnp.zeros((C - 8 * tiles, C), jnp.float32)], axis=0)
        return jnp.transpose(stacked).astype(jnp.bfloat16)

    depth_main = depth_of([bottom[strided(t), :].astype(jnp.float32) for t in range(tiles)])
    depth_side = depth_of([
        jnp.where(lane < C // 2, bottom_side[1, strided(t), :], bottom_side[0, strided(t), :])
        .astype(jnp.float32) for t in range(tiles)])
    row_c = lax.broadcasted_iota(jnp.int32, (C, C), 0)
    chunk = jnp.bitwise_and(lax.broadcasted_iota(jnp.int32, (C, C), 1), 7)
    for t in range(tiles):
        copy_of = jnp.where(row_c == chunk + 8 * t, 1.0, 0.0).astype(jnp.bfloat16)
        main = jnp.dot(depth_main, copy_of, preferred_element_type=jnp.float32)
        beyond = jnp.dot(depth_side, copy_of, preferred_element_type=jnp.float32)
        depth_ref[t, pl.ds(PAD, C), :] = main
        depth_ref[t, pl.ds(0, PAD), :] = beyond[C - PAD:]
        depth_ref[t, pl.ds(PAD + C, PAD), :] = beyond[:PAD]
    lane_level = lax.rem(lax.shift_right_logical(lane, jnp.full_like(lane, 3)), jnp.full_like(lane, levels))
    lane_level = lane_level.astype(jnp.float32)
    for t in range(tiles):
        for k in range(columns):
            ping[t, k] = jnp.where(depth_ref[t, strided_column(k), :] > lane_level, 1.0, 0.0)

    def coefficients(t, k, wet, near):
        gain = SMOOTHING * wet
        gain_ref[t, k] = gain
        keep_ref[t, k] = wet - gain * near

    stencil(ping, coefficients)

    def smooth(source):
        for t in range(tiles):
            for k in range(columns):
                ping[t, k] = jnp.where(gain_ref[t, k] > 0.0, source[t, strided_column(k), :], 0.0)

        def into(target):
            def emit(t, k, v, near):
                target[t, k] = keep_ref[t, k] * v + gain_ref[t, k] * near
            return emit

        def twice(i, carry):
            stencil(ping, into(pong))
            stencil(pong, into(ping))
            return carry

        lax.fori_loop(0, SWEEPS // 2, twice, 0)
        for t in range(tiles):
            for k in range(columns):
                turned_out[t, strided_column(k), :] = ping[t, k]
        turn_back(smooth_ref)

    arrive(field, one_copy, strips)
    smooth(turned_in)
    load_std.wait()
    give.wait_recv()

    def collect(j, carry):
        for f in range(pair):
            for other in range(2):
                if other:
                    p = f * levels + (1 - g) * half + j
                    prior = back_in[f * half + j]
                else:
                    p = f * levels + g * half + j
                    prior = back[(g * pair + f) * half + j]
                x_ref[pl.ds(pl.multiple_of(p * R, R), R), :] = (
                    std[p] * smooth_ref[p, pl.ds(PAD, R), :] + prior)
        return carry

    lax.fori_loop(0, half, collect, 0)
    total = planes * R
    x_ref[pl.ds(total, 8), :] = jnp.zeros((8, C), jnp.float32)
    both = jnp.concatenate([x_ref[pl.ds(0, total), :], x_ref[pl.ds(1, total), :]], axis=1)
    hot = rows_hot[...]
    picked = sum(jnp.dot(hot, part, preferred_element_type=jnp.float32) for part in pieces(both))
    corner_w = corner_hot[...]
    observed = jnp.sum(picked * corner_w, axis=1, keepdims=True)
    misfit = scale * (observed - seen)
    spread = pieces(corner_w * misfit)
    hot_t = rows_hot_t[...]
    scattered = sum(jnp.dot(hot_t, part, preferred_element_type=jnp.float32) for part in spread)
    x_ref[pl.ds(0, total), :] = scattered[:, :C] + pltpu.roll(scattered[:, C:], 1, axis=0)

    def weigh(p, carry):
        wet = deep > lax.rem(p, levels)
        adjoint = x_ref[pl.ds(pl.multiple_of(p * R, R), R), :]
        field_two[p, pl.ds(PAD, R), :] = jnp.where(wet, std[p] * adjoint, 0.0)
        return carry

    lax.fori_loop(0, planes, weigh, 0)
    pack(field_two, strips_out_two)
    start_all(DIRS, two_copy)
    arrive(field_two, two_copy, strips_two)
    smooth(turned_in)

    def write(p, carry):
        out_ref[p] = smooth_ref[p, pl.ds(PAD, R), :]
        return carry

    lax.fori_loop(0, planes, write, 0)
    sent_all(DIRS, bottom_copy)
    sent_all(SIDES, state_copy)
    sent_all(DIRS, one_copy)
    sent_all(DIRS, two_copy)
    give.wait_send()


def body(
    model_state,
    control,
    error_std,
    bottom_level,
    obs_count,
    obs_corner,
    obs_weight,
    obs_value,
    obs_precision,
    *,
    n_zon,
    n_mer,
):
    fields, half, R, C = model_state.shape
    pair, levels = control.shape[:2]
    planes = pair * levels
    slots = obs_corner.shape[-1]
    tiles = (R + 2 * SWEEPS + 7) // 8
    ext = R + 2 * PAD
    state_planes = fields * half
    f32 = jnp.float32
    turned = pltpu.VMEM((tiles, C + 2 * PAD, C), f32)
    slabs = pltpu.VMEM((tiles, (C + 2 * SWEEPS + 7) // 8, 8, C), f32)
    vmem = pl.BlockSpec(memory_space=pltpu.VMEM)
    hbm = pl.BlockSpec(memory_space=pl.ANY)
    dma = pltpu.SemaphoreType.DMA
    sizes = (n_zon, n_mer, levels, half, pair, fields, R, C)
    row_slots = (state_planes + 7) // 8 * 8
    smoothed = pl.pallas_call(
        functools.partial(kernel, sizes),
        out_shape=pltpu.VMEM((planes, R, C), f32),
        in_specs=[hbm] * 9,
        out_specs=vmem,
        scratch_shapes=[
            pltpu.VMEM((R, C), jnp.int32),
            pltpu.VMEM((1, 1), jnp.int32),
            pltpu.VMEM((1, slots), jnp.int32),
            pltpu.VMEM((4, slots), f32),
            pltpu.VMEM((1, slots), f32),
            pltpu.VMEM((1, slots), f32),
            pltpu.VMEM((state_planes, R + 16, C), f32),
            pltpu.VMEM((2, row_slots, C), f32),
            pltpu.VMEM((2, row_slots, C), f32),
            pltpu.VMEM((2, R, C), f32),
            pltpu.VMEM((2, R, C), f32),
            pltpu.VMEM((state_planes, R, C), f32),
            pltpu.VMEM((pair * half, R, C), f32),
            pltpu.VMEM((planes, ext, C), f32),
            turned,
            pltpu.VMEM((2, R, C), f32),
            pltpu.VMEM((2, ext, C), f32),
            pltpu.VMEM((planes, ext, C), f32),
            pltpu.VMEM((2, R, C), f32),
            pltpu.VMEM((2, ext, C), f32),
            pltpu.VMEM((2, C + PAD, C), f32),
            turned,
            turned,
            slabs,
            slabs,
            pltpu.VMEM((ext, C), jnp.int32),
            pltpu.VMEM((2, ext, C), jnp.int32),
            slabs,
            slabs,
            pltpu.VMEM((planes, R, C), f32),
            pltpu.VMEM((planes, ext, C), f32),
            pltpu.VMEM((planes * R + 8, C), f32),
            pltpu.VMEM((slots, planes * R), jnp.bfloat16),
            pltpu.VMEM((planes * R, slots), jnp.bfloat16),
            pltpu.VMEM((128, slots), f32),
            pltpu.VMEM((slots, 2 * C), f32),
            dma((9,)),
            dma((8,)), dma((8,)),
            dma((4,)), dma((4,)),
            dma((8,)), dma((8,)),
            dma((8,)), dma((8,)),
            dma, dma,
        ],
        compiler_params=pltpu.CompilerParams(collective_id=0, has_side_effects=True),
    )(
        model_state.reshape(state_planes, R, C),
        control.reshape(planes, R, C),
        error_std.reshape(planes, R, C),
        bottom_level,
        obs_count.reshape(1, 1),
        obs_corner.reshape(1, slots),
        obs_weight.reshape(4, slots),
        obs_value.reshape(1, slots),
        obs_precision.reshape(1, slots),
    )
    return control + smoothed.reshape(control.shape)


def solution(mesh):
    return jax.shard_map(
        functools.partial(body, n_zon=mesh.shape["zon"], n_mer=mesh.shape["mer"]),
        mesh=mesh,
        in_specs=(
            P(None, "grp", "mer", "zon"),
            P("grp", None, "mer", "zon"),
            P("grp", None, "mer", "zon"),
            P("mer", "zon"),
            P("grp", "mer", "zon"),
            P("grp", "mer", "zon", None),
            P("grp", "mer", "zon", None, None),
            P("grp", "mer", "zon", None),
            P("grp", "mer", "zon", None),
        ),
        out_specs=P("grp", None, "mer", "zon"),
        check_vma=False,
    )
```

```python
import functools

import jax
import jax.numpy as jnp
from jax import lax
from jax.experimental import pallas as pl
from jax.experimental.pallas import tpu as pltpu
from jax.sharding import PartitionSpec as P

SWEEPS = 10
SMOOTHING = 0.2
ADVECTION = 0.1
MIXING = 0.15

MESH = pl.DeviceIdType.MESH
PAD = 16
ZONAL = [(1, 0), (-1, 0)]
MERIDIONAL = [(0, 1), (0, -1)]
SIDES = ZONAL + MERIDIONAL
DIRS = [(1, 1), (1, -1), (-1, 1), (-1, -1)] + ZONAL + MERIDIONAL


def pieces(value):
    parts = []
    for _ in range(2):
        part = value.astype(jnp.bfloat16)
        parts.append(part)
        value = value - part.astype(jnp.float32)
    return parts


def plane_groups(planes, ext, C):
    groups, first, tile = [], 0, 0
    while first < planes:
        count = 1 << ((planes - first).bit_length() - 1)
        chunks = C // count
        groups.append((first, count, tile, chunks, ext // chunks))
        first, tile = first + count, tile + ext // chunks
    return groups


def kernel(
    sizes,
    state_hbm,
    control_hbm,
    std_hbm,
    bottom_hbm,
    count_hbm,
    corner_hbm,
    weight_hbm,
    value_hbm,
    precision_hbm,
    out_ref,
    bottom_ref,
    count_ref,
    corner_ref,
    weight_ref,
    value_ref,
    precision_ref,
    state,
    state_rows,
    state_rows_in,
    state_cols,
    state_cols_in,
    back,
    back_in,
    field,
    strips_out,
    strips,
    field_two,
    strips_out_two,
    strips_two,
    turned_in,
    turned_out,
    depth_ref,
    fold_ref,
    ping,
    pong,
    keep_ref,
    gain_ref,
    bottom,
    bottom_side,
    std,
    smooth_ref,
    x_ref,
    parts_ref,
    rows_hot,
    rows_hot_t,
    obs_stack,
    corner_hot,
    local_sem,
    bot_send,
    bot_recv,
    st_send,
    st_recv,
    one_send,
    one_recv,
    two_send,
    two_recv,
    bg_send,
    bg_recv,
):
    n_zon, n_mer, levels, half, pair, fields, R, C = sizes
    w = SWEEPS
    planes = pair * levels
    ext = R + 2 * PAD
    groups = plane_groups(planes, ext, C)
    total_tiles = sum(tiles for *_, tiles in groups)
    columns = (C + 2 * w + 7) // 8
    column_base = PAD - (8 * columns - C) // 2
    g = lax.axis_index("grp")
    z = lax.axis_index("zon")
    m = lax.axis_index("mer")
    has = {-1: m > 0, 1: m < n_mer - 1}

    def device(dz, dm):
        return (g, lax.rem(z + dz + n_zon, n_zon), m + dm)

    def when(dm, action):
        if dm == 0:
            action()
        else:
            pl.when(has[dm])(action)

    barrier = pltpu.get_barrier_semaphore()
    pl.semaphore_signal(barrier, inc=1, device_id=(1 - g, z, m), device_id_type=MESH)
    for dz, dm in DIRS:
        def greet(dz=dz, dm=dm):
            pl.semaphore_signal(barrier, inc=1, device_id=device(dz, dm), device_id_type=MESH)
        when(dm, greet)

    load_control = pltpu.make_async_copy(control_hbm, smooth_ref.at[:, pl.ds(PAD, R)], local_sem.at[0])
    load_state = pltpu.make_async_copy(state_hbm, state.at[:, pl.ds(8, R)], local_sem.at[1])
    load_std = pltpu.make_async_copy(std_hbm, std, local_sem.at[2])
    load_bottom = pltpu.make_async_copy(bottom_hbm, bottom_ref, local_sem.at[3])
    tables = [
        pltpu.make_async_copy(source, target, local_sem.at[4 + i])
        for i, (source, target) in enumerate([
            (count_hbm, count_ref),
            (corner_hbm, corner_ref),
            (weight_hbm, weight_ref),
            (value_hbm, value_ref),
            (precision_hbm, precision_ref),
        ])
    ]
    load_bottom.start()
    load_state.start()
    load_control.start()
    load_std.start()
    for table in tables:
        table.start()

    lane_r = lax.broadcasted_iota(jnp.int32, (R, C), 1)
    lane = lax.broadcasted_iota(jnp.int32, (8, C), 1)

    def pack(source, target):
        for r in range(R // 8):
            first = jnp.zeros((8, C), jnp.float32)
            last = jnp.zeros((8, C), jnp.float32)
            for p in range(planes):
                at = p * w
                here = (lane >= at) & (lane < at + w)
                u = source[p, pl.ds(PAD + 8 * r, 8), :]
                last = jnp.where(here, pltpu.roll(u, (at + w) % C, axis=1), last)
                first = jnp.where(here, pltpu.roll(u, at, axis=1), first)
            target[0, pl.ds(8 * r, 8), :] = last
            target[1, pl.ds(8 * r, 8), :] = first

    def span(dm):
        if dm == 0:
            return pl.ds(0, R), pl.ds(PAD, R)
        if dm == 1:
            return pl.ds(R - PAD, PAD), pl.ds(0, PAD)
        return pl.ds(0, PAD), pl.ds(PAD + R, PAD)

    def side(dz):
        return 0 if dz == 1 else 1

    def bottom_copy(i):
        dz, dm = DIRS[i]
        src, dst = span(dm)
        target = bottom.at[dst] if dz == 0 else bottom_side.at[side(dz), dst]
        return pltpu.make_async_remote_copy(
            src_ref=bottom_ref.at[src], dst_ref=target,
            send_sem=bot_send.at[i], recv_sem=bot_recv.at[i],
            device_id=device(dz, dm), device_id_type=MESH)

    def halo_copy(i, whole, packed, landed, send, recv):
        dz, dm = DIRS[i]
        src, dst = span(dm)
        if dz == 0:
            inner = pl.ds(PAD + R - w, w) if dm == 1 else pl.ds(PAD, w)
            outer = pl.ds(PAD - w, w) if dm == 1 else pl.ds(PAD + R, w)
            source, target = whole.at[:, inner], whole.at[:, outer]
        else:
            source, target = packed.at[side(dz), src], landed.at[side(dz), dst]
        return pltpu.make_async_remote_copy(
            src_ref=source, dst_ref=target, send_sem=send.at[i], recv_sem=recv.at[i],
            device_id=device(dz, dm), device_id_type=MESH)

    def one_copy(i):
        return halo_copy(i, field, strips_out, strips, one_send, one_recv)

    def two_copy(i):
        return halo_copy(i, field_two, strips_out_two, strips_two, two_send, two_recv)

    def state_copy(i):
        dz, dm = SIDES[i]
        if dz == 0:
            k = 0 if dm == 1 else 1
            source, target = state_rows.at[k], state_rows_in.at[k]
        else:
            source, target = state_cols.at[side(dz)], state_cols_in.at[side(dz)]
        return pltpu.make_async_remote_copy(
            src_ref=source, dst_ref=target, send_sem=st_send.at[i], recv_sem=st_recv.at[i],
            device_id=device(dz, dm), device_id_type=MESH)

    def start_all(copies, make):
        for i, (dz, dm) in enumerate(copies):
            when(dm, lambda i=i: make(i).start())

    def land_all(copies, make):
        for i, (dz, dm) in enumerate(copies):
            when(-dm, lambda i=i: make(i).wait_recv())

    def sent_all(copies, make):
        for i, (dz, dm) in enumerate(copies):
            when(dm, lambda i=i: make(i).wait_send())

    load_bottom.wait()
    bottom[pl.ds(PAD, R)] = bottom_ref[...]
    for dm, rows in ((-1, pl.ds(0, PAD)), (1, pl.ds(PAD + R, PAD))):
        def dry(rows=rows):
            empty = jnp.zeros((PAD, C), jnp.int32)
            bottom[rows] = empty
            bottom_side[0, rows] = empty
            bottom_side[1, rows] = empty
            blank = jnp.zeros((PAD, C), jnp.float32)
            for landed in (strips, strips_two):
                landed[0, rows] = blank
                landed[1, rows] = blank

            def clear(p, carry):
                field[p, rows] = blank
                field_two[p, rows] = blank
                return carry

            lax.fori_loop(0, planes, clear, 0)
        pl.when(jnp.logical_not(has[dm]))(dry)

    load_state.wait()
    first = jnp.zeros((R, C), jnp.float32)
    last = jnp.zeros((R, C), jnp.float32)
    for q in range(fields * half):
        u = state[q, pl.ds(8, R), :]
        last = jnp.where(lane_r == q, pltpu.roll(u, (q + 1) % C, axis=1), last)
        first = jnp.where(lane_r == q, pltpu.roll(u, q, axis=1), first)
        state_rows[0, pl.ds(q, 1), :] = state[q, pl.ds(8 + R - 1, 1), :]
        state_rows[1, pl.ds(q, 1), :] = state[q, pl.ds(8, 1), :]
    state_cols[0] = last
    state_cols[1] = first

    edges = jnp.where(has[-1], 1, 0) + jnp.where(has[1], 1, 0)
    deep = bottom[pl.ds(PAD, R), :]
    load_control.wait()
    for p in range(planes):
        field[p, pl.ds(PAD, R), :] = jnp.where(
            deep > p % levels, smooth_ref[p, pl.ds(PAD, R), :], 0.0)
    pack(field, strips_out)
    pl.semaphore_wait(barrier, 3 + 3 * edges)
    start_all(DIRS, bottom_copy)
    start_all(SIDES, state_copy)
    start_all(DIRS, one_copy)

    for table in tables:
        table.wait()
    shift = C.bit_length() - 1
    slots = corner_ref.shape[1]
    corner = corner_ref[...]
    flat_row = lax.shift_right_logical(corner, jnp.full_like(corner, shift))
    column = corner - flat_row * C
    live = (lax.broadcasted_iota(jnp.int32, (1, slots), 1) < count_ref[...]).astype(jnp.float32)
    obs_stack[...] = jnp.zeros_like(obs_stack)
    obs_stack[pl.ds(0, 1), :] = column.astype(jnp.float32)
    obs_stack[pl.ds(1, 1), :] = flat_row.astype(jnp.float32)
    obs_stack[pl.ds(2, 4), :] = weight_ref[...]
    obs_stack[pl.ds(6, 1), :] = live * precision_ref[...]
    obs_stack[pl.ds(7, 1), :] = value_ref[...]
    turned = jnp.transpose(obs_stack[...])
    col_i = turned[:, 0:1].astype(jnp.int32)
    col_row = turned[:, 1:2].astype(jnp.int32)
    lane_s = lax.broadcasted_iota(jnp.int32, (slots, C), 1)
    here = lane_s == col_i
    beside = lane_s == col_i + 1
    for k in range(2):
        corner_hot[k] = jnp.where(here, turned[:, 2 + 2 * k:3 + 2 * k], 0.0) + jnp.where(
            beside, turned[:, 3 + 2 * k:4 + 2 * k], 0.0)
    scale = turned[:, 6:7]
    seen = turned[:, 7:8]

    def one_hot(k, carry):
        start = pl.multiple_of(k * C, C)
        ids = lax.broadcasted_iota(jnp.int32, (slots, C), 1) + k * C
        ids_t = lax.broadcasted_iota(jnp.int32, (C, slots), 0) + k * C
        for i in range(2):
            rows_hot[i * slots:(i + 1) * slots, pl.ds(start, C)] = jnp.where(
                ids == col_row + i, 1.0, 0.0).astype(jnp.bfloat16)
            rows_hot_t[pl.ds(start, C), i * slots:(i + 1) * slots] = jnp.where(
                ids_t == flat_row + i, 1.0, 0.0).astype(jnp.bfloat16)
        return carry

    lax.fori_loop(0, planes * R // C, one_hot, 0)

    def strided_column(k):
        return pl.ds(column_base + k, 8, columns)

    def turn(source):
        for first, count, tile, chunks, tiles in groups:
            for t in range(tiles):
                rows = [source[first + i, pl.ds(t, chunks, tiles), :] for i in range(count)]
                turned_in[tile + t, pl.ds(PAD, C), :] = jnp.transpose(
                    jnp.concatenate(rows, axis=0))

    def turn_back(target):
        for first, count, tile, chunks, tiles in groups:
            for t in range(tiles):
                rows = jnp.transpose(turned_out[tile + t, pl.ds(PAD, C), :])
                for i in range(count):
                    target[first + i, pl.ds(t, chunks, tiles), :] = rows[chunks * i:chunks * (i + 1)]

    lane_pad = lax.broadcasted_iota(jnp.int32, (PAD, C), 1)

    def unfold(landed):
        for h in range(2):
            for first, count, tile, chunks, tiles in groups:
                bits = chunks.bit_length() - 1
                group = lax.shift_right_logical(lane_pad, jnp.full_like(lane_pad, bits))
                rows = [landed[h, pl.ds(t, chunks, tiles), :] for t in range(tiles)]
                rows.append(jnp.zeros((C - chunks * tiles, C), jnp.float32))
                fold_ref[h, pl.ds(8, C), :] = jnp.transpose(jnp.concatenate(rows, axis=0))
                offset = 8 if h else 8 + w - PAD
                moved = [
                    pltpu.roll(fold_ref[h, pl.ds(offset + (first + i) * w, PAD), :], chunks * i, axis=1)
                    for i in range(count)
                ]
                for t in range(tiles):
                    block = moved[0]
                    for i in range(1, count):
                        block = jnp.where(group == (t + i) % count, moved[i], block)
                    turned_in[tile + t, pl.ds((PAD + C) * h, PAD), :] = pltpu.roll(
                        block, (C - chunks * t) % C, axis=1)

    def stencil(source, emit):
        for first, count, tile, chunks, tiles in groups:
            def column(k):
                return [source[tile + t, k] for t in range(tiles)]

            def lean(u, after):
                beyond = after[1:] + [pltpu.roll(after[0], C - 1, axis=1)]
                return [a + b for a, b in zip(u, beyond)]

            here = column(0)
            wrapped = [pltpu.roll(v, 7, axis=0) for v in here]
            slant_end = lean(column(columns - 1), wrapped)
            slant_before = [pltpu.roll(v, 1, axis=0) for v in slant_end]
            for k in range(columns):
                if k < columns - 1:
                    after = column(k + 1)
                    slant = lean(here, after)
                else:
                    slant = slant_end
                below = [pltpu.roll(slant[-1], 1, axis=1)] + slant[:-1]
                for t in range(tiles):
                    emit(tile + t, k, here[t], below[t] + slant_before[t])
                here, slant_before = after, slant

    def smooth():
        for t in range(total_tiles):
            for k in range(columns):
                ping[t, k] = turned_in[t, strided_column(k), :]

        def into(target):
            def emit(t, k, v, near):
                target[t, k] = keep_ref[t, k] * v + gain_ref[t, k] * near
            return emit

        def twice(i, carry):
            stencil(ping, into(pong))
            stencil(pong, into(ping))
            return carry

        lax.fori_loop(0, SWEEPS // 2, twice, 0)
        for t in range(total_tiles):
            for k in range(columns):
                turned_out[t, strided_column(k), :] = ping[t, k]
        turn_back(smooth_ref)

    def depth_of(rows_of):
        parts = []
        for first, count, tile, chunks, tiles in groups:
            rows = [rows_of(t, chunks, tiles).astype(jnp.float32) for t in range(tiles)]
            rows.append(jnp.zeros((C - chunks * tiles, C), jnp.float32))
            parts.append(jnp.transpose(jnp.concatenate(rows, axis=0)).astype(jnp.bfloat16))
        return parts

    row_c = lax.broadcasted_iota(jnp.int32, (C, C), 0)
    lane_c = lax.broadcasted_iota(jnp.int32, (C, C), 1)

    def spread_depth(parts, emit):
        for part, (first, count, tile, chunks, tiles) in zip(parts, groups):
            chunk = jnp.bitwise_and(lane_c, chunks - 1)
            for t in range(tiles):
                copy_of = jnp.where(row_c == chunk + chunks * t, 1.0, 0.0).astype(jnp.bfloat16)
                emit(tile + t, jnp.dot(part, copy_of, preferred_element_type=jnp.float32))

    lane_level = []
    for first, count, tile, chunks, tiles in groups:
        bits = chunks.bit_length() - 1
        plane = lax.shift_right_logical(lane, jnp.full_like(lane, bits)) + first
        level = jnp.where(plane >= levels, plane - levels, plane)
        lane_level += [level.astype(jnp.float32)] * tiles

    def coefficients():
        def main(t, value):
            depth_ref[t, pl.ds(PAD, C), :] = value

        def beside(t, n, step):
            east = bottom_side[1, pl.ds(t, n, step), :]
            west = bottom_side[0, pl.ds(t, n, step), :]
            at = lax.broadcasted_iota(jnp.int32, (n, C), 1)
            return jnp.where(at < C // 2, east, west)

        def sides(t, value):
            depth_ref[t, pl.ds(0, PAD), :] = value[C - PAD:]
            depth_ref[t, pl.ds(PAD + C, PAD), :] = value[:PAD]

        spread_depth(depth_of(lambda t, n, step: bottom[pl.ds(t, n, step), :]), main)
        spread_depth(depth_of(beside), sides)
        for t in range(total_tiles):
            for k in range(columns):
                pong[t, k] = jnp.where(
                    depth_ref[t, strided_column(k), :] > lane_level[t], 1.0, 0.0)

        def emit(t, k, wet, near):
            gain = SMOOTHING * wet
            gain_ref[t, k] = gain
            keep_ref[t, k] = wet - gain * near

        stencil(pong, emit)

    def meridional(copies, make, only):
        for i, (dz, dm) in enumerate(copies):
            if (dz == 0) == only:
                when(-dm, lambda i=i: make(i).wait_recv())

    share = pair * half
    give = pltpu.make_async_remote_copy(
        src_ref=back.at[pl.ds((1 - g) * share, share)], dst_ref=back_in,
        send_sem=bg_send, recv_sem=bg_recv, device_id=(1 - g, z, m), device_id_type=MESH)

    def model_step():
        land_all(SIDES, state_copy)
        for k, dm, row in ((0, -1, 7), (1, 1, 8 + R)):
            def edge_in(k=k, row=row):
                for q in range(fields * half):
                    state[q, pl.ds(row, 1), :] = state_rows_in[k, pl.ds(q, 1), :]
            def edge_none(row=row):
                for q in range(fields * half):
                    state[q, pl.ds(row, 1), :] = jnp.zeros((1, C), jnp.float32)
            pl.when(has[dm])(edge_in)
            pl.when(jnp.logical_not(has[dm]))(edge_none)

        def neighbours(tile, before, after):
            east = jnp.where(lane_r == C - 1, after, pltpu.roll(tile, C - 1, axis=1))
            west = jnp.where(lane_r == 0, before, pltpu.roll(tile, 1, axis=1))
            return east, west

        east_bottom, west_bottom = neighbours(
            deep,
            pltpu.roll(bottom_side[0, pl.ds(PAD, R), :], 1, axis=1),
            pltpu.roll(bottom_side[1, pl.ds(PAD, R), :], C - 1, axis=1),
        )

        def step_level(j, carry):
            level = g * half + j
            wet_c = (deep > level).astype(jnp.float32)
            wet_e = (east_bottom > level).astype(jnp.float32)
            wet_w = (west_bottom > level).astype(jnp.float32)
            wet_n = (bottom[pl.ds(PAD + 1, R), :] > level).astype(jnp.float32)
            wet_s = (bottom[pl.ds(PAD - 1, R), :] > level).astype(jnp.float32)
            vel_x = state[2 * half + j, pl.ds(8, R), :]
            vel_y = state[3 * half + j, pl.ds(8, R), :]
            for f in range(fields):
                q = f * half + j
                centre = state[q, pl.ds(8, R), :]
                east, west = neighbours(
                    centre,
                    pltpu.roll(state_cols_in[0], lax.rem(C - q, C), axis=1),
                    pltpu.roll(state_cols_in[1], C - 1 - q, axis=1),
                )
                north = state[q, pl.ds(9, R), :]
                south = state[q, pl.ds(7, R), :]
                grad_x = 0.5 * (wet_e * east - wet_w * west)
                grad_y = 0.5 * (wet_n * north - wet_s * south)
                flux = wet_c * (
                    wet_e * (east - centre) + wet_w * (west - centre)
                    + wet_n * (north - centre) + wet_s * (south - centre)
                )
                back[q] = wet_c * (
                    centre - ADVECTION * (vel_x * grad_x + vel_y * grad_y) + MIXING * flux
                )
            return carry

        lax.fori_loop(0, half, step_level, 0)
        give.start()

    meridional(DIRS, one_copy, True)
    turn(field)
    land_all(DIRS, bottom_copy)
    model_step()
    coefficients()
    meridional(DIRS, one_copy, False)
    unfold(strips)
    smooth()
    load_std.wait()
    give.wait_recv()

    def collect(j, carry):
        for f in range(pair):
            for other in range(2):
                if other:
                    p = f * levels + (1 - g) * half + j
                    prior = back_in[f * half + j]
                else:
                    p = f * levels + g * half + j
                    prior = back[(g * pair + f) * half + j]
                rows = pl.ds(pl.multiple_of(p * R, R), R)
                high, low = pieces(std[p] * smooth_ref[p, pl.ds(PAD, R), :] + prior)
                parts_ref[rows, :C] = high
                parts_ref[rows, C:] = low
        return carry

    lax.fori_loop(0, half, collect, 0)
    near_w = corner_hot[0]
    far_w = corner_hot[1]
    picked = jnp.dot(rows_hot[...], parts_ref[...], preferred_element_type=jnp.float32)
    picked = picked[:, :C] + picked[:, C:]
    observed = jnp.sum(picked[:slots] * near_w + picked[slots:] * far_w, axis=1, keepdims=True)
    misfit = scale * (observed - seen)
    spread = jnp.concatenate([near_w * misfit, far_w * misfit], axis=0)
    scattered = jnp.dot(
        rows_hot_t[...], jnp.concatenate(pieces(spread), axis=1), preferred_element_type=jnp.float32)
    x_ref[...] = scattered[:, :C] + scattered[:, C:]

    def weigh(p, carry):
        wet = deep > lax.rem(p, levels)
        adjoint = x_ref[pl.ds(pl.multiple_of(p * R, R), R), :]
        field_two[p, pl.ds(PAD, R), :] = jnp.where(wet, std[p] * adjoint, 0.0)
        return carry

    lax.fori_loop(0, planes, weigh, 0)
    pack(field_two, strips_out_two)
    start_all(DIRS, two_copy)
    meridional(DIRS, two_copy, True)
    turn(field_two)
    meridional(DIRS, two_copy, False)
    unfold(strips_two)
    smooth()

    def write(p, carry):
        out_ref[p] = smooth_ref[p, pl.ds(PAD, R), :]
        return carry

    lax.fori_loop(0, planes, write, 0)
    sent_all(DIRS, bottom_copy)
    sent_all(SIDES, state_copy)
    sent_all(DIRS, one_copy)
    sent_all(DIRS, two_copy)
    give.wait_send()


def body(
    model_state,
    control,
    error_std,
    bottom_level,
    obs_count,
    obs_corner,
    obs_weight,
    obs_value,
    obs_precision,
    *,
    n_zon,
    n_mer,
):
    fields, half, R, C = model_state.shape
    pair, levels = control.shape[:2]
    planes = pair * levels
    slots = obs_corner.shape[-1]
    ext = R + 2 * PAD
    state_planes = fields * half
    f32 = jnp.float32
    total_tiles = sum(tiles for *_, tiles in plane_groups(planes, ext, C))
    turned = pltpu.VMEM((total_tiles, C + 2 * PAD, C), f32)
    slabs = pltpu.VMEM((total_tiles, (C + 2 * SWEEPS + 7) // 8, 8, C), f32)
    vmem = pl.BlockSpec(memory_space=pltpu.VMEM)
    hbm = pl.BlockSpec(memory_space=pl.ANY)
    dma = pltpu.SemaphoreType.DMA
    sizes = (n_zon, n_mer, levels, half, pair, fields, R, C)
    row_slots = (state_planes + 7) // 8 * 8
    smoothed = pl.pallas_call(
        functools.partial(kernel, sizes),
        out_shape=pltpu.VMEM((planes, R, C), f32),
        in_specs=[hbm] * 9,
        out_specs=vmem,
        scratch_shapes=[
            pltpu.VMEM((R, C), jnp.int32),
            pltpu.VMEM((1, 1), jnp.int32),
            pltpu.VMEM((1, slots), jnp.int32),
            pltpu.VMEM((4, slots), f32),
            pltpu.VMEM((1, slots), f32),
            pltpu.VMEM((1, slots), f32),
            pltpu.VMEM((state_planes, R + 16, C), f32),
            pltpu.VMEM((2, row_slots, C), f32),
            pltpu.VMEM((2, row_slots, C), f32),
            pltpu.VMEM((2, R, C), f32),
            pltpu.VMEM((2, R, C), f32),
            pltpu.VMEM((state_planes, R, C), f32),
            pltpu.VMEM((pair * half, R, C), f32),
            pltpu.VMEM((planes, ext, C), f32),
            pltpu.VMEM((2, R, C), f32),
            pltpu.VMEM((2, ext, C), f32),
            pltpu.VMEM((planes, ext, C), f32),
            pltpu.VMEM((2, R, C), f32),
            pltpu.VMEM((2, ext, C), f32),
            turned,
            turned,
            turned,
            pltpu.VMEM((2, C + PAD, C), f32),
            slabs, slabs, slabs, slabs,
            pltpu.VMEM((ext, C), jnp.int32),
            pltpu.VMEM((2, ext, C), jnp.int32),
            pltpu.VMEM((planes, R, C), f32),
            pltpu.VMEM((planes, ext, C), f32),
            pltpu.VMEM((planes * R, C), f32),
            pltpu.VMEM((planes * R, 2 * C), jnp.bfloat16),
            pltpu.VMEM((2 * slots, planes * R), jnp.bfloat16),
            pltpu.VMEM((planes * R, 2 * slots), jnp.bfloat16),
            pltpu.VMEM((128, slots), f32),
            pltpu.VMEM((2, slots, C), f32),
            dma((9,)),
            dma((8,)), dma((8,)),
            dma((4,)), dma((4,)),
            dma((8,)), dma((8,)),
            dma((8,)), dma((8,)),
            dma, dma,
        ],
        compiler_params=pltpu.CompilerParams(collective_id=0, has_side_effects=True),
    )(
        model_state.reshape(state_planes, R, C),
        control.reshape(planes, R, C),
        error_std.reshape(planes, R, C),
        bottom_level,
        obs_count.reshape(1, 1),
        obs_corner.reshape(1, slots),
        obs_weight.reshape(4, slots),
        obs_value.reshape(1, slots),
        obs_precision.reshape(1, slots),
    )
    return control + smoothed.reshape(control.shape)


def solution(mesh):
    return jax.shard_map(
        functools.partial(body, n_zon=mesh.shape["zon"], n_mer=mesh.shape["mer"]),
        mesh=mesh,
        in_specs=(
            P(None, "grp", "mer", "zon"),
            P("grp", None, "mer", "zon"),
            P("grp", None, "mer", "zon"),
            P("mer", "zon"),
            P("grp", "mer", "zon"),
            P("grp", "mer", "zon", None),
            P("grp", "mer", "zon", None, None),
            P("grp", "mer", "zon", None),
            P("grp", "mer", "zon", None),
        ),
        out_specs=P("grp", None, "mer", "zon"),
        check_vma=False,
    )
```

```python
import functools

import jax
import jax.numpy as jnp
from jax import lax
from jax.experimental import pallas as pl
from jax.experimental.pallas import tpu as pltpu
from jax.sharding import PartitionSpec as P

SWEEPS = 10
SMOOTHING = 0.2
ADVECTION = 0.1
MIXING = 0.15

MESH = pl.DeviceIdType.MESH
PAD = 16
ZONAL = [(1, 0), (-1, 0)]
MERIDIONAL = [(0, 1), (0, -1)]
LEDGE = 16
GROUP = 32
DIRS = [(1, 1), (1, -1), (-1, 1), (-1, -1)] + ZONAL + MERIDIONAL


def pieces(value):
    parts = []
    for _ in range(2):
        part = value.astype(jnp.bfloat16)
        parts.append(part)
        value = value - part.astype(jnp.float32)
    return parts


def plane_groups(planes, ext, C):
    groups, first, tile = [], 0, 0
    while first < planes:
        count = 1 << ((planes - first).bit_length() - 1)
        chunks = C // count
        groups.append((first, count, tile, chunks, ext // chunks))
        first, tile = first + count, tile + ext // chunks
    return groups


def kernel(
    sizes,
    state_hbm,
    control_hbm,
    std_hbm,
    bottom_hbm,
    count_hbm,
    corner_hbm,
    weight_hbm,
    value_hbm,
    precision_hbm,
    out_ref,
    bottom_ref,
    count_ref,
    corner_ref,
    weight_ref,
    value_ref,
    precision_ref,
    state,
    state_rows,
    state_rows_in,
    edge_own,
    edge_vel,
    edge_in,
    aux_out,
    aux_in,
    back,
    back_in,
    field,
    strips_out,
    strips,
    field_two,
    strips_out_two,
    strips_two,
    turned_in,
    turned_out,
    depth_ref,
    fold_ref,
    ping,
    pong,
    keep_ref,
    gain_ref,
    bottom,
    bottom_side,
    std,
    smooth_ref,
    x_ref,
    parts_ref,
    rows_hot,
    rows_hot_t,
    obs_stack,
    corner_hot,
    local_sem,
    bot_send,
    bot_recv,
    st_send,
    st_recv,
    one_send,
    one_recv,
    two_send,
    two_recv,
    bg_send,
    bg_recv,
):
    n_zon, n_mer, levels, half, pair, fields, R, C = sizes
    w = SWEEPS
    planes = pair * levels
    ext = R + 2 * PAD
    groups = plane_groups(planes, ext, C)
    total_tiles = sum(tiles for *_, tiles in groups)
    columns = (C + 2 * w + 7) // 8
    column_base = PAD - (8 * columns - C) // 2
    g = lax.axis_index("grp")
    z = lax.axis_index("zon")
    m = lax.axis_index("mer")
    has = {-1: m > 0, 1: m < n_mer - 1}

    def device(dz, dm):
        return (g, lax.rem(z + dz + n_zon, n_zon), m + dm)

    def when(dm, action):
        if dm == 0:
            action()
        else:
            pl.when(has[dm])(action)

    barrier = pltpu.get_barrier_semaphore()
    pl.semaphore_signal(barrier, inc=1, device_id=(1 - g, z, m), device_id_type=MESH)
    for dz, dm in DIRS:
        def greet(dz=dz, dm=dm):
            pl.semaphore_signal(barrier, inc=1, device_id=device(dz, dm), device_id_type=MESH)
        when(dm, greet)

    load_control = pltpu.make_async_copy(control_hbm, smooth_ref.at[:, pl.ds(PAD, R)], local_sem.at[0])
    load_state = pltpu.make_async_copy(state_hbm, state.at[:, pl.ds(8, R)], local_sem.at[1])
    load_std = pltpu.make_async_copy(std_hbm, std, local_sem.at[2])
    load_bottom = pltpu.make_async_copy(bottom_hbm, bottom_ref, local_sem.at[3])
    tables = [
        pltpu.make_async_copy(source, target, local_sem.at[4 + i])
        for i, (source, target) in enumerate([
            (count_hbm, count_ref),
            (corner_hbm, corner_ref),
            (weight_hbm, weight_ref),
            (value_hbm, value_ref),
            (precision_hbm, precision_ref),
        ])
    ]
    load_bottom.start()
    load_state.start()
    load_control.start()
    load_std.start()
    for table in tables:
        table.start()

    lane_r = lax.broadcasted_iota(jnp.int32, (R, C), 1)
    lane = lax.broadcasted_iota(jnp.int32, (8, C), 1)

    def pack(source, target):
        for r in range(R // 8):
            first = jnp.zeros((8, C), jnp.float32)
            last = jnp.zeros((8, C), jnp.float32)
            for p in range(planes):
                at = p * w
                here = (lane >= at) & (lane < at + w)
                u = source[p, pl.ds(PAD + 8 * r, 8), :]
                last = jnp.where(here, pltpu.roll(u, (at + w) % C, axis=1), last)
                first = jnp.where(here, pltpu.roll(u, at, axis=1), first)
            target[0, pl.ds(8 * r, 8), :] = last
            target[1, pl.ds(8 * r, 8), :] = first

    def span(dm):
        if dm == 0:
            return pl.ds(0, R), pl.ds(PAD, R)
        if dm == 1:
            return pl.ds(R - PAD, PAD), pl.ds(0, PAD)
        return pl.ds(0, PAD), pl.ds(PAD + R, PAD)

    def side(dz):
        return 0 if dz == 1 else 1

    def bottom_copy(i):
        dz, dm = DIRS[i]
        src, dst = span(dm)
        if dz == 0:
            source, target = bottom_ref.at[src], bottom.at[dst]
        else:
            source, target = aux_out.at[side(dz)], aux_in.at[3 * side(dz) + dm + 1]
        return pltpu.make_async_remote_copy(
            src_ref=source, dst_ref=target,
            send_sem=bot_send.at[i], recv_sem=bot_recv.at[i],
            device_id=device(dz, dm), device_id_type=MESH)

    def halo_copy(i, whole, packed, landed, send, recv):
        dz, dm = DIRS[i]
        src, dst = span(dm)
        if dz == 0:
            inner = pl.ds(PAD + R - w, w) if dm == 1 else pl.ds(PAD, w)
            outer = pl.ds(PAD - w, w) if dm == 1 else pl.ds(PAD + R, w)
            source, target = whole.at[:, inner], whole.at[:, outer]
        else:
            source, target = packed.at[side(dz), src], landed.at[side(dz), dst]
        return pltpu.make_async_remote_copy(
            src_ref=source, dst_ref=target, send_sem=send.at[i], recv_sem=recv.at[i],
            device_id=device(dz, dm), device_id_type=MESH)

    def one_copy(i):
        return halo_copy(i, field, strips_out, strips, one_send, one_recv)

    def two_copy(i):
        return halo_copy(i, field_two, strips_out_two, strips_two, two_send, two_recv)

    def state_copy(i):
        dz, dm = MERIDIONAL[i]
        k = 0 if dm == 1 else 1
        source, target = state_rows.at[k], state_rows_in.at[k]
        return pltpu.make_async_remote_copy(
            src_ref=source, dst_ref=target, send_sem=st_send.at[i], recv_sem=st_recv.at[i],
            device_id=device(dz, dm), device_id_type=MESH)

    def start_all(copies, make):
        for i, (dz, dm) in enumerate(copies):
            when(dm, lambda i=i: make(i).start())

    def land_all(copies, make):
        for i, (dz, dm) in enumerate(copies):
            when(-dm, lambda i=i: make(i).wait_recv())

    def sent_all(copies, make):
        for i, (dz, dm) in enumerate(copies):
            when(dm, lambda i=i: make(i).wait_send())

    load_bottom.wait()
    bottom[pl.ds(PAD, R)] = bottom_ref[...]
    for dm, rows in ((-1, pl.ds(0, PAD)), (1, pl.ds(PAD + R, PAD))):
        def dry(rows=rows):
            empty = jnp.zeros((PAD, C), jnp.int32)
            bottom[rows] = empty
            bottom_side[0, rows] = empty
            bottom_side[1, rows] = empty
            blank = jnp.zeros((PAD, C), jnp.float32)
            for landed in (strips, strips_two):
                landed[0, rows] = blank
                landed[1, rows] = blank

            def clear(p, carry):
                field[p, rows] = blank
                field_two[p, rows] = blank
                return carry

            lax.fori_loop(0, planes, clear, 0)
        pl.when(jnp.logical_not(has[dm]))(dry)

    load_state.wait()
    first = jnp.zeros((R, C), jnp.float32)
    last = jnp.zeros((R, C), jnp.float32)
    for q in range(fields * half):
        u = state[q, pl.ds(8, R), :]
        last = jnp.where(lane_r == q, pltpu.roll(u, (q + 1) % C, axis=1), last)
        first = jnp.where(lane_r == q, pltpu.roll(u, q, axis=1), first)
        state_rows[0, pl.ds(q, 1), :] = state[q, pl.ds(8 + R - 1, 1), :]
        state_rows[1, pl.ds(q, 1), :] = state[q, pl.ds(8, 1), :]
    fold = C // GROUP
    depth_here = bottom_ref[...].astype(jnp.float32)
    holds_depth = (lane_r >= LEDGE) & (lane_r < LEDGE + w)
    edge_own[0] = jnp.where(holds_depth, pltpu.roll(depth_here, (LEDGE + w) % C, axis=1), last)
    edge_own[1] = jnp.where(holds_depth, pltpu.roll(depth_here, LEDGE, axis=1), first)
    for k in range(2):
        aux_out[k] = sum(
            pltpu.roll(edge_own[k, pl.ds(h * (R // fold), R // fold), :], GROUP * h, axis=1)
            for h in range(fold))

    edges = jnp.where(has[-1], 1, 0) + jnp.where(has[1], 1, 0)
    deep = bottom[pl.ds(PAD, R), :]
    load_control.wait()
    for p in range(planes):
        field[p, pl.ds(PAD, R), :] = jnp.where(
            deep > p % levels, smooth_ref[p, pl.ds(PAD, R), :], 0.0)
    pack(field, strips_out)
    pl.semaphore_wait(barrier, 3 + 3 * edges)
    start_all(DIRS, bottom_copy)
    start_all(MERIDIONAL, state_copy)
    start_all(DIRS, one_copy)

    for table in tables:
        table.wait()
    shift = C.bit_length() - 1
    slots = corner_ref.shape[1]
    corner = corner_ref[...]
    flat_row = lax.shift_right_logical(corner, jnp.full_like(corner, shift))
    column = corner - flat_row * C
    live = (lax.broadcasted_iota(jnp.int32, (1, slots), 1) < count_ref[...]).astype(jnp.float32)
    obs_stack[...] = jnp.zeros_like(obs_stack)
    obs_stack[pl.ds(0, 1), :] = column.astype(jnp.float32)
    obs_stack[pl.ds(1, 1), :] = flat_row.astype(jnp.float32)
    obs_stack[pl.ds(2, 4), :] = weight_ref[...]
    obs_stack[pl.ds(6, 1), :] = live * precision_ref[...]
    obs_stack[pl.ds(7, 1), :] = value_ref[...]
    turned = jnp.transpose(obs_stack[...])
    col_i = turned[:, 0:1].astype(jnp.int32)
    col_row = turned[:, 1:2].astype(jnp.int32)
    lane_s = lax.broadcasted_iota(jnp.int32, (slots, C), 1)
    here = lane_s == col_i
    beside = lane_s == col_i + 1
    for k in range(2):
        corner_hot[k] = jnp.where(here, turned[:, 2 + 2 * k:3 + 2 * k], 0.0) + jnp.where(
            beside, turned[:, 3 + 2 * k:4 + 2 * k], 0.0)
    scale = turned[:, 6:7]
    seen = turned[:, 7:8]

    def one_hot(k, carry):
        start = pl.multiple_of(k * C, C)
        ids = lax.broadcasted_iota(jnp.int32, (slots, C), 1) + k * C
        ids_t = lax.broadcasted_iota(jnp.int32, (C, slots), 0) + k * C
        for i in range(2):
            rows_hot[i * slots:(i + 1) * slots, pl.ds(start, C)] = jnp.where(
                ids == col_row + i, 1.0, 0.0).astype(jnp.bfloat16)
            rows_hot_t[pl.ds(start, C), i * slots:(i + 1) * slots] = jnp.where(
                ids_t == flat_row + i, 1.0, 0.0).astype(jnp.bfloat16)
        return carry

    lax.fori_loop(0, planes * R // C, one_hot, 0)

    def strided_column(k):
        return pl.ds(column_base + k, 8, columns)

    def turn(source):
        for first, count, tile, chunks, tiles in groups:
            for t in range(tiles):
                rows = [source[first + i, pl.ds(t, chunks, tiles), :] for i in range(count)]
                turned_in[tile + t, pl.ds(PAD, C), :] = jnp.transpose(
                    jnp.concatenate(rows, axis=0))

    def turn_back(target):
        for first, count, tile, chunks, tiles in groups:
            for t in range(tiles):
                rows = jnp.transpose(turned_out[tile + t, pl.ds(PAD, C), :])
                for i in range(count):
                    target[first + i, pl.ds(t, chunks, tiles), :] = rows[chunks * i:chunks * (i + 1)]

    lane_pad = lax.broadcasted_iota(jnp.int32, (PAD, C), 1)

    def unfold(landed):
        for h in range(2):
            for first, count, tile, chunks, tiles in groups:
                bits = chunks.bit_length() - 1
                group = lax.shift_right_logical(lane_pad, jnp.full_like(lane_pad, bits))
                rows = [landed[h, pl.ds(t, chunks, tiles), :] for t in range(tiles)]
                rows.append(jnp.zeros((C - chunks * tiles, C), jnp.float32))
                fold_ref[h, pl.ds(8, C), :] = jnp.transpose(jnp.concatenate(rows, axis=0))
                offset = 8 if h else 8 + w - PAD
                moved = [
                    pltpu.roll(fold_ref[h, pl.ds(offset + (first + i) * w, PAD), :], chunks * i, axis=1)
                    for i in range(count)
                ]
                for t in range(tiles):
                    block = moved[0]
                    for i in range(1, count):
                        block = jnp.where(group == (t + i) % count, moved[i], block)
                    turned_in[tile + t, pl.ds((PAD + C) * h, PAD), :] = pltpu.roll(
                        block, (C - chunks * t) % C, axis=1)

    def stencil(source, emit):
        for first, count, tile, chunks, tiles in groups:
            def column(k):
                return [source[tile + t, k] for t in range(tiles)]

            def lean(u, after):
                beyond = after[1:] + [pltpu.roll(after[0], C - 1, axis=1)]
                return [a + b for a, b in zip(u, beyond)]

            here = column(0)
            wrapped = [pltpu.roll(v, 7, axis=0) for v in here]
            slant_end = lean(column(columns - 1), wrapped)
            slant_before = [pltpu.roll(v, 1, axis=0) for v in slant_end]
            for k in range(columns):
                if k < columns - 1:
                    after = column(k + 1)
                    slant = lean(here, after)
                else:
                    slant = slant_end
                below = [pltpu.roll(slant[-1], 1, axis=1)] + slant[:-1]
                for t in range(tiles):
                    emit(tile + t, k, here[t], below[t] + slant_before[t])
                here, slant_before = after, slant

    def smooth():
        for t in range(total_tiles):
            for k in range(columns):
                ping[t, k] = turned_in[t, strided_column(k), :]

        def into(target):
            def emit(t, k, v, near):
                target[t, k] = keep_ref[t, k] * v + gain_ref[t, k] * near
            return emit

        def twice(i, carry):
            stencil(ping, into(pong))
            stencil(pong, into(ping))
            return carry

        lax.fori_loop(0, SWEEPS // 2, twice, 0)
        for t in range(total_tiles):
            for k in range(columns):
                turned_out[t, strided_column(k), :] = ping[t, k]
        turn_back(smooth_ref)

    def depth_of(rows_of):
        parts = []
        for first, count, tile, chunks, tiles in groups:
            rows = [rows_of(t, chunks, tiles).astype(jnp.float32) for t in range(tiles)]
            rows.append(jnp.zeros((C - chunks * tiles, C), jnp.float32))
            parts.append(jnp.transpose(jnp.concatenate(rows, axis=0)).astype(jnp.bfloat16))
        return parts

    row_c = lax.broadcasted_iota(jnp.int32, (C, C), 0)
    lane_c = lax.broadcasted_iota(jnp.int32, (C, C), 1)

    def spread_depth(parts, emit):
        for part, (first, count, tile, chunks, tiles) in zip(parts, groups):
            chunk = jnp.bitwise_and(lane_c, chunks - 1)
            for t in range(tiles):
                copy_of = jnp.where(row_c == chunk + chunks * t, 1.0, 0.0).astype(jnp.bfloat16)
                emit(tile + t, jnp.dot(part, copy_of, preferred_element_type=jnp.float32))

    lane_level = []
    for first, count, tile, chunks, tiles in groups:
        bits = chunks.bit_length() - 1
        plane = lax.shift_right_logical(lane, jnp.full_like(lane, bits)) + first
        level = jnp.where(plane >= levels, plane - levels, plane)
        lane_level += [level.astype(jnp.float32)] * tiles

    def coefficients_main():
        def main(t, value):
            depth_ref[t, pl.ds(PAD, C), :] = value

        spread_depth(depth_of(lambda t, n, step: bottom[pl.ds(t, n, step), :]), main)

    def coefficients():
        def beside(t, n, step):
            east = bottom_side[1, pl.ds(t, n, step), :]
            west = bottom_side[0, pl.ds(t, n, step), :]
            at = lax.broadcasted_iota(jnp.int32, (n, C), 1)
            return jnp.where(at < C // 2, east, west)

        def sides(t, value):
            depth_ref[t, pl.ds(0, PAD), :] = value[C - PAD:]
            depth_ref[t, pl.ds(PAD + C, PAD), :] = value[:PAD]

        spread_depth(depth_of(beside), sides)
        for t in range(total_tiles):
            for k in range(columns):
                pong[t, k] = jnp.where(
                    depth_ref[t, strided_column(k), :] > lane_level[t], 1.0, 0.0)

        def emit(t, k, wet, near):
            gain = SMOOTHING * wet
            gain_ref[t, k] = gain
            keep_ref[t, k] = wet - gain * near

        stencil(pong, emit)

    def meridional(copies, make, only):
        for i, (dz, dm) in enumerate(copies):
            if (dz == 0) == only:
                when(-dm, lambda i=i: make(i).wait_recv())

    share = pair * half
    give = pltpu.make_async_remote_copy(
        src_ref=back.at[pl.ds((1 - g) * share, share)], dst_ref=back_in,
        send_sem=bg_send, recv_sem=bg_recv, device_id=(1 - g, z, m), device_id_type=MESH)

    def model_step():
        land_all(MERIDIONAL, state_copy)
        for k, dm, row in ((0, -1, 7), (1, 1, 8 + R)):
            def edge_in(k=k, row=row):
                for q in range(fields * half):
                    state[q, pl.ds(row, 1), :] = state_rows_in[k, pl.ds(q, 1), :]
            def edge_none(row=row):
                for q in range(fields * half):
                    state[q, pl.ds(row, 1), :] = jnp.zeros((1, C), jnp.float32)
            pl.when(has[dm])(edge_in)
            pl.when(jnp.logical_not(has[dm]))(edge_none)

        east_bottom = jnp.where(lane_r == C - 1, 0, pltpu.roll(deep, C - 1, axis=1))
        west_bottom = jnp.where(lane_r == 0, 0, pltpu.roll(deep, 1, axis=1))

        def step_level(j, carry):
            level = g * half + j
            wet_c = (deep > level).astype(jnp.float32)
            wet_e = (east_bottom > level).astype(jnp.float32)
            wet_w = (west_bottom > level).astype(jnp.float32)
            wet_n = (bottom[pl.ds(PAD + 1, R), :] > level).astype(jnp.float32)
            wet_s = (bottom[pl.ds(PAD - 1, R), :] > level).astype(jnp.float32)
            vel_x = state[2 * half + j, pl.ds(8, R), :]
            vel_y = state[3 * half + j, pl.ds(8, R), :]
            for f in range(fields):
                q = f * half + j
                centre = state[q, pl.ds(8, R), :]
                east = pltpu.roll(centre, C - 1, axis=1)
                west = pltpu.roll(centre, 1, axis=1)
                north = state[q, pl.ds(9, R), :]
                south = state[q, pl.ds(7, R), :]
                grad_x = 0.5 * (wet_e * east - wet_w * west)
                grad_y = 0.5 * (wet_n * north - wet_s * south)
                flux = wet_c * (
                    wet_e * (east - centre) + wet_w * (west - centre)
                    + wet_n * (north - centre) + wet_s * (south - centre)
                )
                back[q] = wet_c * (
                    centre - ADVECTION * (vel_x * grad_x + vel_y * grad_y) + MIXING * flux
                )
            return carry

        lax.fori_loop(0, half, step_level, 0)
        for k in range(2):
            vel = edge_own[k]
            speed = jnp.zeros((R, C), jnp.float32)
            for f in range(fields):
                speed = jnp.where(
                    lane_r >= f * half, pltpu.roll(vel, (C + (f - 2) * half) % C, axis=1), speed)
            edge_vel[k] = speed

    def edge_step():
        rows = R // fold
        for k in range(2):
            move = C - w - LEDGE if k == 0 else C - LEDGE
            middle = aux_in[3 * k + 1]
            for h in range(fold):
                edge_in[k, pl.ds(h * rows, rows), :] = pltpu.roll(
                    middle, (C - GROUP * h) % C, axis=1)
                bottom_side[k, pl.ds(PAD + h * rows, rows), :] = pltpu.roll(
                    middle, (C + move - GROUP * h) % C, axis=1).astype(jnp.int32)
            for dm, h, start in ((1, fold - 1, 0), (-1, 0, PAD + R)):
                def corner(dm=dm, h=h, start=start, k=k, move=move):
                    bottom_side[k, pl.ds(start, rows), :] = pltpu.roll(
                        aux_in[3 * k + dm + 1], (C + move - GROUP * h) % C, axis=1).astype(jnp.int32)
                when(-dm, corner)
        level_at = lane_r
        for f in range(1, fields):
            level_at = jnp.where(lane_r >= f * half, lane_r - f * half, level_at)
        level_at = (level_at + g * half).astype(jnp.float32)
        corrections = []
        for k in range(2):
            near_lane, own_lane = (LEDGE + w - 1, LEDGE) if k == 0 else (LEDGE, LEDGE + w - 1)
            beyond = edge_in[k]
            own = edge_own[1 - k]
            both = (beyond[:, near_lane:near_lane + 1] > level_at) & (
                own[:, own_lane:own_lane + 1] > level_at)
            drift = (0.5 * ADVECTION if k == 0 else -0.5 * ADVECTION) * edge_vel[1 - k]
            corrections.append(jnp.where(both, (MIXING + drift) * beyond - MIXING * own, 0.0))
        for q in range(fields * half):
            back[q] = back[q] + jnp.where(
                lane_r == 0, pltpu.roll(corrections[0], (C - q) % C, axis=1),
                jnp.where(
                    lane_r == C - 1, pltpu.roll(corrections[1], C - 1 - q, axis=1), 0.0))
        give.start()

    meridional(DIRS, bottom_copy, True)
    model_step()
    coefficients_main()
    meridional(DIRS, one_copy, True)
    turn(field)
    meridional(DIRS, bottom_copy, False)
    edge_step()
    coefficients()
    meridional(DIRS, one_copy, False)
    unfold(strips)
    smooth()
    load_std.wait()
    give.wait_recv()

    def collect(j, carry):
        for f in range(pair):
            for other in range(2):
                if other:
                    p = f * levels + (1 - g) * half + j
                    prior = back_in[f * half + j]
                else:
                    p = f * levels + g * half + j
                    prior = back[(g * pair + f) * half + j]
                rows = pl.ds(pl.multiple_of(p * R, R), R)
                high, low = pieces(std[p] * smooth_ref[p, pl.ds(PAD, R), :] + prior)
                parts_ref[rows, :C] = high
                parts_ref[rows, C:] = low
        return carry

    lax.fori_loop(0, half, collect, 0)
    near_w = corner_hot[0]
    far_w = corner_hot[1]
    picked = jnp.dot(rows_hot[...], parts_ref[...], preferred_element_type=jnp.float32)
    picked = picked[:, :C] + picked[:, C:]
    observed = jnp.sum(picked[:slots] * near_w + picked[slots:] * far_w, axis=1, keepdims=True)
    misfit = scale * (observed - seen)
    spread = jnp.concatenate([near_w * misfit, far_w * misfit], axis=0)
    scattered = jnp.dot(
        rows_hot_t[...], jnp.concatenate(pieces(spread), axis=1), preferred_element_type=jnp.float32)
    x_ref[...] = scattered[:, :C] + scattered[:, C:]

    def weigh(p, carry):
        wet = deep > lax.rem(p, levels)
        adjoint = x_ref[pl.ds(pl.multiple_of(p * R, R), R), :]
        field_two[p, pl.ds(PAD, R), :] = jnp.where(wet, std[p] * adjoint, 0.0)
        return carry

    lax.fori_loop(0, planes, weigh, 0)
    pack(field_two, strips_out_two)
    start_all(DIRS, two_copy)
    meridional(DIRS, two_copy, True)
    turn(field_two)
    meridional(DIRS, two_copy, False)
    unfold(strips_two)
    smooth()

    def write(p, carry):
        out_ref[p] = smooth_ref[p, pl.ds(PAD, R), :]
        return carry

    lax.fori_loop(0, planes, write, 0)
    sent_all(DIRS, bottom_copy)
    sent_all(MERIDIONAL, state_copy)
    sent_all(DIRS, one_copy)
    sent_all(DIRS, two_copy)
    give.wait_send()


def body(
    model_state,
    control,
    error_std,
    bottom_level,
    obs_count,
    obs_corner,
    obs_weight,
    obs_value,
    obs_precision,
    *,
    n_zon,
    n_mer,
):
    fields, half, R, C = model_state.shape
    pair, levels = control.shape[:2]
    planes = pair * levels
    slots = obs_corner.shape[-1]
    ext = R + 2 * PAD
    state_planes = fields * half
    f32 = jnp.float32
    total_tiles = sum(tiles for *_, tiles in plane_groups(planes, ext, C))
    turned = pltpu.VMEM((total_tiles, C + 2 * PAD, C), f32)
    slabs = pltpu.VMEM((total_tiles, (C + 2 * SWEEPS + 7) // 8, 8, C), f32)
    vmem = pl.BlockSpec(memory_space=pltpu.VMEM)
    hbm = pl.BlockSpec(memory_space=pl.ANY)
    dma = pltpu.SemaphoreType.DMA
    sizes = (n_zon, n_mer, levels, half, pair, fields, R, C)
    row_slots = (state_planes + 7) // 8 * 8
    smoothed = pl.pallas_call(
        functools.partial(kernel, sizes),
        out_shape=pltpu.VMEM((planes, R, C), f32),
        in_specs=[hbm] * 9,
        out_specs=vmem,
        scratch_shapes=[
            pltpu.VMEM((R, C), jnp.int32),
            pltpu.VMEM((1, 1), jnp.int32),
            pltpu.VMEM((1, slots), jnp.int32),
            pltpu.VMEM((4, slots), f32),
            pltpu.VMEM((1, slots), f32),
            pltpu.VMEM((1, slots), f32),
            pltpu.VMEM((state_planes, R + 16, C), f32),
            pltpu.VMEM((2, row_slots, C), f32),
            pltpu.VMEM((2, row_slots, C), f32),
            pltpu.VMEM((2, R, C), f32),
            pltpu.VMEM((2, R, C), f32),
            pltpu.VMEM((2, R, C), f32),
            pltpu.VMEM((2, R * GROUP // C, C), f32),
            pltpu.VMEM((6, R * GROUP // C, C), f32),
            pltpu.VMEM((state_planes, R, C), f32),
            pltpu.VMEM((pair * half, R, C), f32),
            pltpu.VMEM((planes, ext, C), f32),
            pltpu.VMEM((2, R, C), f32),
            pltpu.VMEM((2, ext, C), f32),
            pltpu.VMEM((planes, ext, C), f32),
            pltpu.VMEM((2, R, C), f32),
            pltpu.VMEM((2, ext, C), f32),
            turned,
            turned,
            turned,
            pltpu.VMEM((2, C + PAD, C), f32),
            slabs, slabs, slabs, slabs,
            pltpu.VMEM((ext, C), jnp.int32),
            pltpu.VMEM((2, ext, C), jnp.int32),
            pltpu.VMEM((planes, R, C), f32),
            pltpu.VMEM((planes, ext, C), f32),
            pltpu.VMEM((planes * R, C), f32),
            pltpu.VMEM((planes * R, 2 * C), jnp.bfloat16),
            pltpu.VMEM((2 * slots, planes * R), jnp.bfloat16),
            pltpu.VMEM((planes * R, 2 * slots), jnp.bfloat16),
            pltpu.VMEM((128, slots), f32),
            pltpu.VMEM((2, slots, C), f32),
            dma((9,)),
            dma((8,)), dma((8,)),
            dma((2,)), dma((2,)),
            dma((8,)), dma((8,)),
            dma((8,)), dma((8,)),
            dma, dma,
        ],
        compiler_params=pltpu.CompilerParams(collective_id=0, has_side_effects=True),
    )(
        model_state.reshape(state_planes, R, C),
        control.reshape(planes, R, C),
        error_std.reshape(planes, R, C),
        bottom_level,
        obs_count.reshape(1, 1),
        obs_corner.reshape(1, slots),
        obs_weight.reshape(4, slots),
        obs_value.reshape(1, slots),
        obs_precision.reshape(1, slots),
    )
    return control + smoothed.reshape(control.shape)


def solution(mesh):
    return jax.shard_map(
        functools.partial(body, n_zon=mesh.shape["zon"], n_mer=mesh.shape["mer"]),
        mesh=mesh,
        in_specs=(
            P(None, "grp", "mer", "zon"),
            P("grp", None, "mer", "zon"),
            P("grp", None, "mer", "zon"),
            P("mer", "zon"),
            P("grp", "mer", "zon"),
            P("grp", "mer", "zon", None),
            P("grp", "mer", "zon", None, None),
            P("grp", "mer", "zon", None),
            P("grp", "mer", "zon", None),
        ),
        out_specs=P("grp", None, "mer", "zon"),
        check_vma=False,
    )
```

```python
import functools

import jax
import jax.numpy as jnp
from jax import lax
from jax.experimental import pallas as pl
from jax.experimental.pallas import tpu as pltpu
from jax.sharding import PartitionSpec as P

SWEEPS = 10
SMOOTHING = 0.2
ADVECTION = 0.1
MIXING = 0.15

MESH = pl.DeviceIdType.MESH
PAD = 16
ZONAL = [(1, 0), (-1, 0)]
MERIDIONAL = [(0, 1), (0, -1)]
LEDGE = 16
GROUP = 32
DIRS = [(1, 1), (1, -1), (-1, 1), (-1, -1)] + ZONAL + MERIDIONAL


def pieces(value):
    parts = []
    for _ in range(2):
        part = value.astype(jnp.bfloat16)
        parts.append(part)
        value = value - part.astype(jnp.float32)
    return parts


def kernel(
    sizes,
    state_hbm,
    control_hbm,
    std_hbm,
    bottom_hbm,
    count_hbm,
    corner_hbm,
    weight_hbm,
    value_hbm,
    precision_hbm,
    out_ref,
    bottom_ref,
    count_ref,
    corner_ref,
    weight_ref,
    value_ref,
    precision_ref,
    state,
    state_rows,
    state_rows_in,
    edge_own,
    edge_vel,
    edge_in,
    aux_out,
    aux_in,
    back,
    back_in,
    field,
    strips_out,
    strips,
    field_two,
    strips_out_two,
    strips_two,
    mixed,
    turned_in,
    turned_out,
    depth_ref,
    fold_ref,
    moved_ref,
    owner_ref,
    ping,
    pong,
    keep_ref,
    gain_ref,
    bottom,
    bottom_side,
    std,
    smooth_ref,
    x_ref,
    parts_ref,
    rows_hot,
    rows_hot_t,
    obs_stack,
    corner_hot,
    local_sem,
    bot_send,
    bot_recv,
    st_send,
    st_recv,
    one_send,
    one_recv,
    two_send,
    two_recv,
    bg_send,
    bg_recv,
):
    n_zon, n_mer, levels, half, pair, fields, R, C = sizes
    w = SWEEPS
    planes = pair * levels
    ext = R + 2 * PAD
    chunks = C // planes
    tiles = (R + 2 * w + chunks - 1) // chunks
    base = PAD - (chunks * tiles - R) // 2
    columns = (C + 2 * w + 7) // 8
    column_base = PAD - (8 * columns - C) // 2
    g = lax.axis_index("grp")
    z = lax.axis_index("zon")
    m = lax.axis_index("mer")
    has = {-1: m > 0, 1: m < n_mer - 1}

    def device(dz, dm):
        return (g, lax.rem(z + dz + n_zon, n_zon), m + dm)

    def when(dm, action):
        if dm == 0:
            action()
        else:
            pl.when(has[dm])(action)

    barrier = pltpu.get_barrier_semaphore()
    pl.semaphore_signal(barrier, inc=1, device_id=(1 - g, z, m), device_id_type=MESH)
    for dz, dm in DIRS:
        def greet(dz=dz, dm=dm):
            pl.semaphore_signal(barrier, inc=1, device_id=device(dz, dm), device_id_type=MESH)
        when(dm, greet)

    load_control = pltpu.make_async_copy(control_hbm, smooth_ref.at[:, pl.ds(PAD, R)], local_sem.at[0])
    load_state = pltpu.make_async_copy(state_hbm, state.at[:, pl.ds(8, R)], local_sem.at[1])
    load_std = pltpu.make_async_copy(std_hbm, std, local_sem.at[2])
    load_bottom = pltpu.make_async_copy(bottom_hbm, bottom_ref, local_sem.at[3])
    tables = [
        pltpu.make_async_copy(source, target, local_sem.at[4 + i])
        for i, (source, target) in enumerate([
            (count_hbm, count_ref),
            (corner_hbm, corner_ref),
            (weight_hbm, weight_ref),
            (value_hbm, value_ref),
            (precision_hbm, precision_ref),
        ])
    ]
    load_bottom.start()
    load_state.start()
    load_control.start()
    load_std.start()
    for table in tables:
        table.start()

    lane_r = lax.broadcasted_iota(jnp.int32, (R, C), 1)
    lane = lax.broadcasted_iota(jnp.int32, (8, C), 1)

    def pack(source, target):
        place = [(lane >= p * w) & (lane < p * w + w) for p in range(planes + 1)]
        place[planes] = place[planes] | (lane < (planes + 1) * w - C)
        for r in range(R // 8):
            first = jnp.zeros((8, C), jnp.float32)
            last = jnp.zeros((8, C), jnp.float32)
            for p in range(planes):
                u = pltpu.roll(source[p, pl.ds(PAD + 8 * r, 8), :], (p * w + w) % C, axis=1)
                last = jnp.where(place[p], u, last)
                first = jnp.where(place[p + 1], u, first)
            target[0, pl.ds(8 * r, 8), :] = last
            target[1, pl.ds(8 * r, 8), :] = first

    def span(dm):
        if dm == 0:
            return pl.ds(0, R), pl.ds(PAD, R)
        if dm == 1:
            return pl.ds(R - PAD, PAD), pl.ds(0, PAD)
        return pl.ds(0, PAD), pl.ds(PAD + R, PAD)

    def side(dz):
        return 0 if dz == 1 else 1

    def bottom_copy(i):
        dz, dm = DIRS[i]
        src, dst = span(dm)
        if dz == 0:
            source, target = bottom_ref.at[src], bottom.at[dst]
        else:
            source, target = aux_out.at[side(dz)], aux_in.at[3 * side(dz) + dm + 1]
        return pltpu.make_async_remote_copy(
            src_ref=source, dst_ref=target,
            send_sem=bot_send.at[i], recv_sem=bot_recv.at[i],
            device_id=device(dz, dm), device_id_type=MESH)

    def halo_copy(i, whole, packed, landed, send, recv):
        dz, dm = DIRS[i]
        src, dst = span(dm)
        if dz == 0:
            inner = pl.ds(PAD + R - w, w) if dm == 1 else pl.ds(PAD, w)
            outer = pl.ds(PAD - w, w) if dm == 1 else pl.ds(PAD + R, w)
            source, target = whole.at[:, inner], whole.at[:, outer]
        else:
            source, target = packed.at[side(dz), src], landed.at[side(dz), dst]
        return pltpu.make_async_remote_copy(
            src_ref=source, dst_ref=target, send_sem=send.at[i], recv_sem=recv.at[i],
            device_id=device(dz, dm), device_id_type=MESH)

    def one_copy(i):
        return halo_copy(i, field, strips_out, strips, one_send, one_recv)

    def two_copy(i):
        return halo_copy(i, field_two, strips_out_two, strips_two, two_send, two_recv)

    def state_copy(i):
        dz, dm = MERIDIONAL[i]
        k = 0 if dm == 1 else 1
        source, target = state_rows.at[k], state_rows_in.at[k]
        return pltpu.make_async_remote_copy(
            src_ref=source, dst_ref=target, send_sem=st_send.at[i], recv_sem=st_recv.at[i],
            device_id=device(dz, dm), device_id_type=MESH)

    def start_all(copies, make):
        for i, (dz, dm) in enumerate(copies):
            when(dm, lambda i=i: make(i).start())

    def land_all(copies, make):
        for i, (dz, dm) in enumerate(copies):
            when(-dm, lambda i=i: make(i).wait_recv())

    def sent_all(copies, make):
        for i, (dz, dm) in enumerate(copies):
            when(dm, lambda i=i: make(i).wait_send())

    load_bottom.wait()
    bottom[pl.ds(PAD, R)] = bottom_ref[...]
    for dm, rows in ((-1, pl.ds(0, PAD)), (1, pl.ds(PAD + R, PAD))):
        def dry(rows=rows):
            empty = jnp.zeros((PAD, C), jnp.int32)
            bottom[rows] = empty
            bottom_side[0, rows] = empty
            bottom_side[1, rows] = empty
            blank = jnp.zeros((PAD, C), jnp.float32)
            for landed in (strips, strips_two):
                landed[0, rows] = blank
                landed[1, rows] = blank

            def clear(p, carry):
                field[p, rows] = blank
                field_two[p, rows] = blank
                return carry

            lax.fori_loop(0, planes, clear, 0)
        pl.when(jnp.logical_not(has[dm]))(dry)

    load_state.wait()
    first = jnp.zeros((R, C), jnp.float32)
    last = jnp.zeros((R, C), jnp.float32)
    for q in range(fields * half):
        u = state[q, pl.ds(8, R), :]
        last = jnp.where(lane_r == q, pltpu.roll(u, (q + 1) % C, axis=1), last)
        first = jnp.where(lane_r == q, pltpu.roll(u, q, axis=1), first)
        state_rows[0, pl.ds(q, 1), :] = state[q, pl.ds(8 + R - 1, 1), :]
        state_rows[1, pl.ds(q, 1), :] = state[q, pl.ds(8, 1), :]
    fold = C // GROUP
    depth_here = bottom_ref[...].astype(jnp.float32)
    holds_depth = (lane_r >= LEDGE) & (lane_r < LEDGE + w)
    edge_own[0] = jnp.where(holds_depth, pltpu.roll(depth_here, (LEDGE + w) % C, axis=1), last)
    edge_own[1] = jnp.where(holds_depth, pltpu.roll(depth_here, LEDGE, axis=1), first)
    for k in range(2):
        aux_out[k] = sum(
            pltpu.roll(edge_own[k, pl.ds(h * (R // fold), R // fold), :], GROUP * h, axis=1)
            for h in range(fold))

    edges = jnp.where(has[-1], 1, 0) + jnp.where(has[1], 1, 0)
    deep = bottom[pl.ds(PAD, R), :]
    load_control.wait()
    for p in range(planes):
        field[p, pl.ds(PAD, R), :] = jnp.where(
            deep > p % levels, smooth_ref[p, pl.ds(PAD, R), :], 0.0)
    pack(field, strips_out)
    pl.semaphore_wait(barrier, 3 + 3 * edges)
    start_all(DIRS, bottom_copy)
    start_all(MERIDIONAL, state_copy)
    start_all(DIRS, one_copy)

    for table in tables:
        table.wait()
    shift = C.bit_length() - 1
    slots = corner_ref.shape[1]
    corner = corner_ref[...]
    flat_row = lax.shift_right_logical(corner, jnp.full_like(corner, shift))
    column = corner - flat_row * C
    live = (lax.broadcasted_iota(jnp.int32, (1, slots), 1) < count_ref[...]).astype(jnp.float32)
    obs_stack[...] = jnp.zeros_like(obs_stack)
    obs_stack[pl.ds(0, 1), :] = column.astype(jnp.float32)
    obs_stack[pl.ds(1, 1), :] = flat_row.astype(jnp.float32)
    obs_stack[pl.ds(2, 4), :] = weight_ref[...]
    obs_stack[pl.ds(6, 1), :] = live * precision_ref[...]
    obs_stack[pl.ds(7, 1), :] = value_ref[...]
    turned = jnp.transpose(obs_stack[...])
    col_i = turned[:, 0:1].astype(jnp.int32)
    col_row = turned[:, 1:2].astype(jnp.int32)
    lane_s = lax.broadcasted_iota(jnp.int32, (slots, C), 1)
    here = lane_s == col_i
    beside = lane_s == col_i + 1
    for k in range(2):
        corner_hot[k] = jnp.where(here, turned[:, 2 + 2 * k:3 + 2 * k], 0.0) + jnp.where(
            beside, turned[:, 3 + 2 * k:4 + 2 * k], 0.0)
    scale = turned[:, 6:7]
    seen = turned[:, 7:8]

    def one_hot(k, carry):
        start = pl.multiple_of(k * C, C)
        ids = lax.broadcasted_iota(jnp.int32, (slots, C), 1) + k * C
        ids_t = lax.broadcasted_iota(jnp.int32, (C, slots), 0) + k * C
        for i in range(2):
            rows_hot[i * slots:(i + 1) * slots, pl.ds(start, C)] = jnp.where(
                ids == col_row + i, 1.0, 0.0).astype(jnp.bfloat16)
            rows_hot_t[pl.ds(start, C), i * slots:(i + 1) * slots] = jnp.where(
                ids_t == flat_row + i, 1.0, 0.0).astype(jnp.bfloat16)
        return carry

    lax.fori_loop(0, planes * R // C, one_hot, 0)

    def strided_column(k):
        return pl.ds(column_base + k, 8, columns)

    def rows_at(t):
        return pl.ds(base + t, chunks, tiles)

    def turn(source):
        for t in range(tiles):
            for p in range(planes):
                mixed[t, pl.ds(chunks * p, chunks), :] = source[p, rows_at(t), :]
            turned_in[t, pl.ds(PAD, C), :] = jnp.transpose(mixed[t])

    def turn_back(target):
        for t in range(tiles):
            mixed[t] = jnp.transpose(turned_out[t, pl.ds(PAD, C), :])
            for p in range(planes):
                target[p, rows_at(t), :] = mixed[t, pl.ds(chunks * p, chunks), :]

    def plane_of(at):
        plane = jnp.zeros_like(at)
        for p in range(1, planes):
            plane = jnp.where(at >= chunks * p, p, plane)
        return plane

    for t in range(tiles):
        owner_ref[t] = plane_of(jnp.bitwise_and(lane + (C - chunks * t), C - 1))

    def unfold(landed):
        for h in range(2):
            for t in range(tiles):
                mixed[h, pl.ds(chunks * t, chunks), :] = landed[h, rows_at(t), :]
            folded = jnp.transpose(mixed[h])
            fold_ref[h, pl.ds(8, C), :] = folded
            fold_ref[h, pl.ds(8 + C, 8), :] = folded[:8]
            offset = 8 + w if h else 8 + w - PAD
            for p in range(planes):
                moved_ref[h, p] = pltpu.roll(
                    fold_ref[h, pl.ds(offset + p * w, PAD), :], chunks * p, axis=1)
        for t in range(tiles):
            owner = owner_ref[t]
            mine = [owner == p for p in range(planes)]
            for h in range(2):
                for part in range(0, PAD, 8):
                    block = moved_ref[h, 0, pl.ds(part, 8), :]
                    for p in range(1, planes):
                        block = jnp.where(mine[p], moved_ref[h, p, pl.ds(part, 8), :], block)
                    turned_in[t, pl.ds((PAD + C) * h + part, 8), :] = pltpu.roll(
                        block, (C - chunks * t) % C, axis=1)

    def stencil(source, emit):
        def column(k):
            return [source[t, k] for t in range(tiles)]

        def lean(u, after):
            beyond = after[1:] + [pltpu.roll(after[0], C - 1, axis=1)]
            return [a + b for a, b in zip(u, beyond)]

        here = column(0)
        wrapped = [pltpu.roll(v, 7, axis=0) for v in here]
        slant_end = lean(column(columns - 1), wrapped)
        slant_before = [pltpu.roll(v, 1, axis=0) for v in slant_end]
        for k in range(columns):
            if k < columns - 1:
                after = column(k + 1)
                slant = lean(here, after)
            else:
                slant = slant_end
            below = [pltpu.roll(slant[-1], 1, axis=1)] + slant[:-1]
            for t in range(tiles):
                emit(t, k, here[t], below[t] + slant_before[t])
            here, slant_before = after, slant

    def smooth():
        for t in range(tiles):
            for k in range(columns):
                ping[t, k] = turned_in[t, strided_column(k), :]

        def into(target):
            def emit(t, k, v, near):
                target[t, k] = keep_ref[t, k] * v + gain_ref[t, k] * near
            return emit

        def twice(i, carry):
            stencil(ping, into(pong))
            stencil(pong, into(ping))
            return carry

        lax.fori_loop(0, SWEEPS // 2, twice, 0)
        for t in range(tiles):
            for k in range(columns):
                turned_out[t, strided_column(k), :] = ping[t, k]
        turn_back(smooth_ref)

    def depth_of(rows_of):
        for t in range(tiles):
            mixed[0, pl.ds(chunks * t, chunks), :] = rows_of(rows_at(t)).astype(jnp.float32)
        spare = C - chunks * tiles
        mixed[0, pl.ds(chunks * tiles, spare), :] = jnp.zeros((spare, C), jnp.float32)
        return jnp.transpose(mixed[0]).astype(jnp.bfloat16)

    row_c = lax.broadcasted_iota(jnp.int32, (C, C), 0)
    lane_c = lax.broadcasted_iota(jnp.int32, (C, C), 1)
    chunk_c = lane_c - chunks * plane_of(lane_c)

    def spread_depth(part, emit):
        for t in range(tiles):
            copy_of = jnp.where(row_c == chunk_c + chunks * t, 1.0, 0.0).astype(jnp.bfloat16)
            emit(t, jnp.dot(part, copy_of, preferred_element_type=jnp.float32))

    plane = plane_of(lane)
    lane_level = jnp.where(plane >= levels, plane - levels, plane).astype(jnp.float32)

    def coefficients_main():
        def main(t, value):
            depth_ref[t, pl.ds(PAD, C), :] = value

        spread_depth(depth_of(lambda rows: bottom[rows, :]), main)

    def coefficients():
        def beside(rows):
            east = bottom_side[1, rows, :]
            west = bottom_side[0, rows, :]
            at = lax.broadcasted_iota(jnp.int32, (chunks, C), 1)
            return jnp.where(at < C // 2, east, west)

        def sides(t, value):
            depth_ref[t, pl.ds(0, PAD), :] = value[C - PAD:]
            depth_ref[t, pl.ds(PAD + C, PAD), :] = value[:PAD]

        spread_depth(depth_of(beside), sides)
        for t in range(tiles):
            for k in range(columns):
                pong[t, k] = jnp.where(
                    depth_ref[t, strided_column(k), :] > lane_level, 1.0, 0.0)

        def emit(t, k, wet, near):
            gain = SMOOTHING * wet
            gain_ref[t, k] = gain
            keep_ref[t, k] = wet - gain * near

        stencil(pong, emit)

    def meridional(copies, make, only):
        for i, (dz, dm) in enumerate(copies):
            if (dz == 0) == only:
                when(-dm, lambda i=i: make(i).wait_recv())

    share = pair * half
    give = pltpu.make_async_remote_copy(
        src_ref=back.at[pl.ds((1 - g) * share, share)], dst_ref=back_in,
        send_sem=bg_send, recv_sem=bg_recv, device_id=(1 - g, z, m), device_id_type=MESH)

    def model_step():
        land_all(MERIDIONAL, state_copy)
        for k, dm, row in ((0, -1, 7), (1, 1, 8 + R)):
            def edge_in(k=k, row=row):
                for q in range(fields * half):
                    state[q, pl.ds(row, 1), :] = state_rows_in[k, pl.ds(q, 1), :]
            def edge_none(row=row):
                for q in range(fields * half):
                    state[q, pl.ds(row, 1), :] = jnp.zeros((1, C), jnp.float32)
            pl.when(has[dm])(edge_in)
            pl.when(jnp.logical_not(has[dm]))(edge_none)

        east_bottom = jnp.where(lane_r == C - 1, 0, pltpu.roll(deep, C - 1, axis=1))
        west_bottom = jnp.where(lane_r == 0, 0, pltpu.roll(deep, 1, axis=1))

        def step_level(j, carry):
            level = g * half + j
            wet_c = (deep > level).astype(jnp.float32)
            wet_e = (east_bottom > level).astype(jnp.float32)
            wet_w = (west_bottom > level).astype(jnp.float32)
            wet_n = (bottom[pl.ds(PAD + 1, R), :] > level).astype(jnp.float32)
            wet_s = (bottom[pl.ds(PAD - 1, R), :] > level).astype(jnp.float32)
            vel_x = state[2 * half + j, pl.ds(8, R), :]
            vel_y = state[3 * half + j, pl.ds(8, R), :]
            for f in range(fields):
                q = f * half + j
                centre = state[q, pl.ds(8, R), :]
                east = pltpu.roll(centre, C - 1, axis=1)
                west = pltpu.roll(centre, 1, axis=1)
                north = state[q, pl.ds(9, R), :]
                south = state[q, pl.ds(7, R), :]
                grad_x = 0.5 * (wet_e * east - wet_w * west)
                grad_y = 0.5 * (wet_n * north - wet_s * south)
                flux = wet_c * (
                    wet_e * (east - centre) + wet_w * (west - centre)
                    + wet_n * (north - centre) + wet_s * (south - centre)
                )
                back[q] = wet_c * (
                    centre - ADVECTION * (vel_x * grad_x + vel_y * grad_y) + MIXING * flux
                )
            return carry

        lax.fori_loop(0, half, step_level, 0)
        for k in range(2):
            vel = edge_own[k]
            speed = jnp.zeros((R, C), jnp.float32)
            for f in range(fields):
                speed = jnp.where(
                    lane_r >= f * half, pltpu.roll(vel, (C + (f - 2) * half) % C, axis=1), speed)
            edge_vel[k] = speed

    def edge_step():
        rows = R // fold
        for k in range(2):
            move = C - w - LEDGE if k == 0 else C - LEDGE
            middle = aux_in[3 * k + 1]
            for h in range(fold):
                edge_in[k, pl.ds(h * rows, rows), :] = pltpu.roll(
                    middle, (C - GROUP * h) % C, axis=1)
                bottom_side[k, pl.ds(PAD + h * rows, rows), :] = pltpu.roll(
                    middle, (C + move - GROUP * h) % C, axis=1).astype(jnp.int32)
            for dm, h, start in ((1, fold - 1, 0), (-1, 0, PAD + R)):
                def corner(dm=dm, h=h, start=start, k=k, move=move):
                    bottom_side[k, pl.ds(start, rows), :] = pltpu.roll(
                        aux_in[3 * k + dm + 1], (C + move - GROUP * h) % C, axis=1).astype(jnp.int32)
                when(-dm, corner)
        level_at = lane_r
        for f in range(1, fields):
            level_at = jnp.where(lane_r >= f * half, lane_r - f * half, level_at)
        level_at = (level_at + g * half).astype(jnp.float32)
        corrections = []
        for k in range(2):
            near_lane, own_lane = (LEDGE + w - 1, LEDGE) if k == 0 else (LEDGE, LEDGE + w - 1)
            beyond = edge_in[k]
            own = edge_own[1 - k]
            both = (beyond[:, near_lane:near_lane + 1] > level_at) & (
                own[:, own_lane:own_lane + 1] > level_at)
            drift = (0.5 * ADVECTION if k == 0 else -0.5 * ADVECTION) * edge_vel[1 - k]
            corrections.append(jnp.where(both, (MIXING + drift) * beyond - MIXING * own, 0.0))
        for q in range(fields * half):
            back[q] = back[q] + jnp.where(
                lane_r == 0, pltpu.roll(corrections[0], (C - q) % C, axis=1),
                jnp.where(
                    lane_r == C - 1, pltpu.roll(corrections[1], C - 1 - q, axis=1), 0.0))
        give.start()

    meridional(DIRS, bottom_copy, True)
    model_step()
    coefficients_main()
    meridional(DIRS, one_copy, True)
    turn(field)
    meridional(DIRS, bottom_copy, False)
    edge_step()
    coefficients()
    meridional(DIRS, one_copy, False)
    unfold(strips)
    smooth()
    load_std.wait()
    give.wait_recv()

    def collect(j, carry):
        for f in range(pair):
            for other in range(2):
                if other:
                    p = f * levels + (1 - g) * half + j
                    prior = back_in[f * half + j]
                else:
                    p = f * levels + g * half + j
                    prior = back[(g * pair + f) * half + j]
                rows = pl.ds(pl.multiple_of(p * R, R), R)
                high, low = pieces(std[p] * smooth_ref[p, pl.ds(PAD, R), :] + prior)
                parts_ref[rows, :C] = high
                parts_ref[rows, C:] = low
        return carry

    lax.fori_loop(0, half, collect, 0)
    near_w = corner_hot[0]
    far_w = corner_hot[1]
    picked = jnp.dot(rows_hot[...], parts_ref[...], preferred_element_type=jnp.float32)
    picked = picked[:, :C] + picked[:, C:]
    observed = jnp.sum(picked[:slots] * near_w + picked[slots:] * far_w, axis=1, keepdims=True)
    misfit = scale * (observed - seen)
    spread = jnp.concatenate([near_w * misfit, far_w * misfit], axis=0)
    scattered = jnp.dot(
        rows_hot_t[...], jnp.concatenate(pieces(spread), axis=1), preferred_element_type=jnp.float32)
    x_ref[...] = scattered[:, :C] + scattered[:, C:]

    def weigh(p, carry):
        wet = deep > lax.rem(p, levels)
        adjoint = x_ref[pl.ds(pl.multiple_of(p * R, R), R), :]
        field_two[p, pl.ds(PAD, R), :] = jnp.where(wet, std[p] * adjoint, 0.0)
        return carry

    lax.fori_loop(0, planes, weigh, 0)
    pack(field_two, strips_out_two)
    start_all(DIRS, two_copy)
    meridional(DIRS, two_copy, True)
    turn(field_two)
    meridional(DIRS, two_copy, False)
    unfold(strips_two)
    smooth()

    def write(p, carry):
        out_ref[p] = smooth_ref[p, pl.ds(PAD, R), :]
        return carry

    lax.fori_loop(0, planes, write, 0)
    sent_all(DIRS, bottom_copy)
    sent_all(MERIDIONAL, state_copy)
    sent_all(DIRS, one_copy)
    sent_all(DIRS, two_copy)
    give.wait_send()


def body(
    model_state,
    control,
    error_std,
    bottom_level,
    obs_count,
    obs_corner,
    obs_weight,
    obs_value,
    obs_precision,
    *,
    n_zon,
    n_mer,
):
    fields, half, R, C = model_state.shape
    pair, levels = control.shape[:2]
    planes = pair * levels
    slots = obs_corner.shape[-1]
    ext = R + 2 * PAD
    state_planes = fields * half
    f32 = jnp.float32
    chunks = C // planes
    tiles = (R + 2 * SWEEPS + chunks - 1) // chunks
    turned = pltpu.VMEM((tiles, C + 2 * PAD, C), f32)
    slabs = pltpu.VMEM((tiles, (C + 2 * SWEEPS + 7) // 8, 8, C), f32)
    vmem = pl.BlockSpec(memory_space=pltpu.VMEM)
    hbm = pl.BlockSpec(memory_space=pl.ANY)
    dma = pltpu.SemaphoreType.DMA
    sizes = (n_zon, n_mer, levels, half, pair, fields, R, C)
    row_slots = (state_planes + 7) // 8 * 8
    smoothed = pl.pallas_call(
        functools.partial(kernel, sizes),
        out_shape=pltpu.VMEM((planes, R, C), f32),
        in_specs=[hbm] * 9,
        out_specs=vmem,
        scratch_shapes=[
            pltpu.VMEM((R, C), jnp.int32),
            pltpu.VMEM((1, 1), jnp.int32),
            pltpu.VMEM((1, slots), jnp.int32),
            pltpu.VMEM((4, slots), f32),
            pltpu.VMEM((1, slots), f32),
            pltpu.VMEM((1, slots), f32),
            pltpu.VMEM((state_planes, R + 16, C), f32),
            pltpu.VMEM((2, row_slots, C), f32),
            pltpu.VMEM((2, row_slots, C), f32),
            pltpu.VMEM((2, R, C), f32),
            pltpu.VMEM((2, R, C), f32),
            pltpu.VMEM((2, R, C), f32),
            pltpu.VMEM((2, R * GROUP // C, C), f32),
            pltpu.VMEM((6, R * GROUP // C, C), f32),
            pltpu.VMEM((state_planes, R, C), f32),
            pltpu.VMEM((pair * half, R, C), f32),
            pltpu.VMEM((planes, ext, C), f32),
            pltpu.VMEM((2, R, C), f32),
            pltpu.VMEM((2, ext, C), f32),
            pltpu.VMEM((planes, ext, C), f32),
            pltpu.VMEM((2, R, C), f32),
            pltpu.VMEM((2, ext, C), f32),
            pltpu.VMEM((tiles, C, C), f32),
            turned,
            turned,
            turned,
            pltpu.VMEM((2, C + PAD, C), f32),
            pltpu.VMEM((2, planes, PAD, C), f32),
            pltpu.VMEM((tiles, 8, C), jnp.int32),
            slabs, slabs, slabs, slabs,
            pltpu.VMEM((ext, C), jnp.int32),
            pltpu.VMEM((2, ext, C), jnp.int32),
            pltpu.VMEM((planes, R, C), f32),
            pltpu.VMEM((planes, ext, C), f32),
            pltpu.VMEM((planes * R, C), f32),
            pltpu.VMEM((planes * R, 2 * C), jnp.bfloat16),
            pltpu.VMEM((2 * slots, planes * R), jnp.bfloat16),
            pltpu.VMEM((planes * R, 2 * slots), jnp.bfloat16),
            pltpu.VMEM((128, slots), f32),
            pltpu.VMEM((2, slots, C), f32),
            dma((9,)),
            dma((8,)), dma((8,)),
            dma((2,)), dma((2,)),
            dma((8,)), dma((8,)),
            dma((8,)), dma((8,)),
            dma, dma,
        ],
        compiler_params=pltpu.CompilerParams(collective_id=0, has_side_effects=True),
    )(
        model_state.reshape(state_planes, R, C),
        control.reshape(planes, R, C),
        error_std.reshape(planes, R, C),
        bottom_level,
        obs_count.reshape(1, 1),
        obs_corner.reshape(1, slots),
        obs_weight.reshape(4, slots),
        obs_value.reshape(1, slots),
        obs_precision.reshape(1, slots),
    )
    return control + smoothed.reshape(control.shape)


def solution(mesh):
    return jax.shard_map(
        functools.partial(body, n_zon=mesh.shape["zon"], n_mer=mesh.shape["mer"]),
        mesh=mesh,
        in_specs=(
            P(None, "grp", "mer", "zon"),
            P("grp", None, "mer", "zon"),
            P("grp", None, "mer", "zon"),
            P("mer", "zon"),
            P("grp", "mer", "zon"),
            P("grp", "mer", "zon", None),
            P("grp", "mer", "zon", None, None),
            P("grp", "mer", "zon", None),
            P("grp", "mer", "zon", None),
        ),
        out_specs=P("grp", None, "mer", "zon"),
        check_vma=False,
    )
```

```python
import functools

import jax
import jax.numpy as jnp
from jax import lax
from jax.experimental import pallas as pl
from jax.experimental.pallas import tpu as pltpu
from jax.sharding import PartitionSpec as P

SWEEPS = 10
SMOOTHING = 0.2
ADVECTION = 0.1
MIXING = 0.15

MESH = pl.DeviceIdType.MESH
PAD = 16
ZONAL = [(1, 0), (-1, 0)]
MERIDIONAL = [(0, 1), (0, -1)]
LEDGE = 16
GROUP = 32
DIRS = [(1, 1), (1, -1), (-1, 1), (-1, -1)] + ZONAL + MERIDIONAL


def pieces(value):
    parts = []
    for _ in range(2):
        part = value.astype(jnp.bfloat16)
        parts.append(part)
        value = value - part.astype(jnp.float32)
    return parts


def kernel(
    sizes,
    state_hbm,
    control_hbm,
    std_hbm,
    bottom_hbm,
    count_hbm,
    corner_hbm,
    weight_hbm,
    value_hbm,
    precision_hbm,
    out_ref,
    bottom_ref,
    count_ref,
    corner_ref,
    weight_ref,
    value_ref,
    precision_ref,
    state,
    state_rows,
    state_rows_in,
    edge_own,
    edge_vel,
    edge_in,
    aux_out,
    aux_in,
    back,
    back_in,
    field,
    strips_out,
    strips,
    field_two,
    strips_out_two,
    strips_two,
    mixed,
    turned_in,
    turned_out,
    depth_ref,
    fold_ref,
    moved_ref,
    owner_ref,
    ping,
    pong,
    keep_ref,
    gain_ref,
    bottom,
    bottom_side,
    std,
    smooth_ref,
    x_ref,
    parts_ref,
    rows_hot,
    rows_hot_t,
    obs_stack,
    corner_hot,
    local_sem,
    bot_send,
    bot_recv,
    st_send,
    st_recv,
    one_send,
    one_recv,
    two_send,
    two_recv,
    bg_send,
    bg_recv,
):
    n_zon, n_mer, levels, half, pair, fields, R, C = sizes
    w = SWEEPS
    planes = pair * levels
    ext = R + 2 * PAD
    chunks = C // planes
    tiles = (R + 2 * w + chunks - 1) // chunks
    base = PAD - (chunks * tiles - R) // 2
    columns = (C + 2 * w + 7) // 8
    column_base = PAD - (8 * columns - C) // 2
    g = lax.axis_index("grp")
    z = lax.axis_index("zon")
    m = lax.axis_index("mer")
    has = {-1: m > 0, 1: m < n_mer - 1}

    def device(dz, dm):
        return (g, lax.rem(z + dz + n_zon, n_zon), m + dm)

    def when(dm, action):
        if dm == 0:
            action()
        else:
            pl.when(has[dm])(action)

    barrier = pltpu.get_barrier_semaphore()
    pl.semaphore_signal(barrier, inc=1, device_id=(1 - g, z, m), device_id_type=MESH)
    for dz, dm in DIRS:
        def greet(dz=dz, dm=dm):
            pl.semaphore_signal(barrier, inc=1, device_id=device(dz, dm), device_id_type=MESH)
        when(dm, greet)

    load_control = pltpu.make_async_copy(control_hbm, smooth_ref.at[:, pl.ds(PAD, R)], local_sem.at[0])
    load_state = pltpu.make_async_copy(state_hbm, state.at[:, pl.ds(8, R)], local_sem.at[1])
    load_std = pltpu.make_async_copy(std_hbm, std, local_sem.at[2])
    load_bottom = pltpu.make_async_copy(bottom_hbm, bottom_ref, local_sem.at[3])
    tables = [
        pltpu.make_async_copy(source, target, local_sem.at[4 + i])
        for i, (source, target) in enumerate([
            (count_hbm, count_ref),
            (corner_hbm, corner_ref),
            (weight_hbm, weight_ref),
            (value_hbm, value_ref),
            (precision_hbm, precision_ref),
        ])
    ]
    load_bottom.start()
    load_state.start()
    load_control.start()
    load_std.start()
    for table in tables:
        table.start()

    lane_r = lax.broadcasted_iota(jnp.int32, (R, C), 1)
    lane = lax.broadcasted_iota(jnp.int32, (8, C), 1)

    def pack(source, target, blocks):
        place = [(lane >= p * w) & (lane < p * w + w) for p in range(planes + 1)]
        place[planes] = place[planes] | (lane < (planes + 1) * w - C)
        for r in blocks:
            first = jnp.zeros((8, C), jnp.float32)
            last = jnp.zeros((8, C), jnp.float32)
            for p in range(planes):
                u = pltpu.roll(source[p, pl.ds(PAD + 8 * r, 8), :], (p * w + w) % C, axis=1)
                last = jnp.where(place[p], u, last)
                first = jnp.where(place[p + 1], u, first)
            target[0, pl.ds(8 * r, 8), :] = last
            target[1, pl.ds(8 * r, 8), :] = first

    def span(dm):
        if dm == 0:
            return pl.ds(0, R), pl.ds(PAD, R)
        if dm == 1:
            return pl.ds(R - PAD, PAD), pl.ds(0, PAD)
        return pl.ds(0, PAD), pl.ds(PAD + R, PAD)

    def side(dz):
        return 0 if dz == 1 else 1

    def bottom_copy(i):
        dz, dm = DIRS[i]
        src, dst = span(dm)
        if dz == 0:
            source, target = bottom_ref.at[src], bottom.at[dst]
        else:
            source, target = aux_out.at[side(dz)], aux_in.at[3 * side(dz) + dm + 1]
        return pltpu.make_async_remote_copy(
            src_ref=source, dst_ref=target,
            send_sem=bot_send.at[i], recv_sem=bot_recv.at[i],
            device_id=device(dz, dm), device_id_type=MESH)

    def halo_copy(i, whole, packed, landed, send, recv):
        dz, dm = DIRS[i]
        src, dst = span(dm)
        if dz == 0:
            inner = pl.ds(PAD + R - w, w) if dm == 1 else pl.ds(PAD, w)
            outer = pl.ds(PAD - w, w) if dm == 1 else pl.ds(PAD + R, w)
            source, target = whole.at[:, inner], whole.at[:, outer]
        else:
            source, target = packed.at[side(dz), src], landed.at[side(dz), dst]
        return pltpu.make_async_remote_copy(
            src_ref=source, dst_ref=target, send_sem=send.at[i], recv_sem=recv.at[i],
            device_id=device(dz, dm), device_id_type=MESH)

    def one_copy(i):
        return halo_copy(i, field, strips_out, strips, one_send, one_recv)

    def two_copy(i):
        return halo_copy(i, field_two, strips_out_two, strips_two, two_send, two_recv)

    def state_copy(i):
        dz, dm = MERIDIONAL[i]
        k = 0 if dm == 1 else 1
        source, target = state_rows.at[k], state_rows_in.at[k]
        return pltpu.make_async_remote_copy(
            src_ref=source, dst_ref=target, send_sem=st_send.at[i], recv_sem=st_recv.at[i],
            device_id=device(dz, dm), device_id_type=MESH)

    def start_all(copies, make):
        for i, (dz, dm) in enumerate(copies):
            when(dm, lambda i=i: make(i).start())

    def land_all(copies, make):
        for i, (dz, dm) in enumerate(copies):
            when(-dm, lambda i=i: make(i).wait_recv())

    def sent_all(copies, make):
        for i, (dz, dm) in enumerate(copies):
            when(dm, lambda i=i: make(i).wait_send())

    load_bottom.wait()
    bottom[pl.ds(PAD, R)] = bottom_ref[...]
    for dm, rows in ((-1, pl.ds(0, PAD)), (1, pl.ds(PAD + R, PAD))):
        def dry(rows=rows):
            empty = jnp.zeros((PAD, C), jnp.int32)
            bottom[rows] = empty
            bottom_side[0, rows] = empty
            bottom_side[1, rows] = empty
            blank = jnp.zeros((PAD, C), jnp.float32)
            for landed in (strips, strips_two):
                landed[0, rows] = blank
                landed[1, rows] = blank

            def clear(p, carry):
                field[p, rows] = blank
                field_two[p, rows] = blank
                return carry

            lax.fori_loop(0, planes, clear, 0)
        pl.when(jnp.logical_not(has[dm]))(dry)

    load_state.wait()
    first = jnp.zeros((R, C), jnp.float32)
    last = jnp.zeros((R, C), jnp.float32)
    for q in range(fields * half):
        u = state[q, pl.ds(8, R), :]
        last = jnp.where(lane_r == q, pltpu.roll(u, (q + 1) % C, axis=1), last)
        first = jnp.where(lane_r == q, pltpu.roll(u, q, axis=1), first)
        state_rows[0, pl.ds(q, 1), :] = state[q, pl.ds(8 + R - 1, 1), :]
        state_rows[1, pl.ds(q, 1), :] = state[q, pl.ds(8, 1), :]
    fold = C // GROUP
    depth_here = bottom_ref[...].astype(jnp.float32)
    holds_depth = (lane_r >= LEDGE) & (lane_r < LEDGE + w)
    edge_own[0] = jnp.where(holds_depth, pltpu.roll(depth_here, (LEDGE + w) % C, axis=1), last)
    edge_own[1] = jnp.where(holds_depth, pltpu.roll(depth_here, LEDGE, axis=1), first)
    for k in range(2):
        aux_out[k] = sum(
            pltpu.roll(edge_own[k, pl.ds(h * (R // fold), R // fold), :], GROUP * h, axis=1)
            for h in range(fold))

    edges = jnp.where(has[-1], 1, 0) + jnp.where(has[1], 1, 0)
    deep = bottom[pl.ds(PAD, R), :]
    load_control.wait()
    for p in range(planes):
        field[p, pl.ds(PAD, R), :] = jnp.where(
            deep > p % levels, smooth_ref[p, pl.ds(PAD, R), :], 0.0)
    pack(field, strips_out, range(R // 8))
    pl.semaphore_wait(barrier, 3 + 3 * edges)
    start_all(DIRS, bottom_copy)
    start_all(MERIDIONAL, state_copy)
    start_all(DIRS, one_copy)

    for table in tables:
        table.wait()
    shift = C.bit_length() - 1
    slots = corner_ref.shape[1]
    corner = corner_ref[...]
    flat_row = lax.shift_right_logical(corner, jnp.full_like(corner, shift))
    column = corner - flat_row * C
    live = (lax.broadcasted_iota(jnp.int32, (1, slots), 1) < count_ref[...]).astype(jnp.float32)
    obs_stack[...] = jnp.zeros_like(obs_stack)
    obs_stack[pl.ds(0, 1), :] = column.astype(jnp.float32)
    obs_stack[pl.ds(1, 1), :] = flat_row.astype(jnp.float32)
    obs_stack[pl.ds(2, 4), :] = weight_ref[...]
    obs_stack[pl.ds(6, 1), :] = live * precision_ref[...]
    obs_stack[pl.ds(7, 1), :] = value_ref[...]
    turned = jnp.transpose(obs_stack[...])
    col_i = turned[:, 0:1].astype(jnp.int32)
    col_row = turned[:, 1:2].astype(jnp.int32)
    lane_s = lax.broadcasted_iota(jnp.int32, (slots, C), 1)
    here = lane_s == col_i
    beside = lane_s == col_i + 1
    for k in range(2):
        corner_hot[k] = jnp.where(here, turned[:, 2 + 2 * k:3 + 2 * k], 0.0) + jnp.where(
            beside, turned[:, 3 + 2 * k:4 + 2 * k], 0.0)
    scale = turned[:, 6:7]
    seen = turned[:, 7:8]

    def one_hot(k, carry):
        start = pl.multiple_of(k * C, C)
        ids = lax.broadcasted_iota(jnp.int32, (slots, C), 1) + k * C
        ids_t = lax.broadcasted_iota(jnp.int32, (C, slots), 0) + k * C
        for i in range(2):
            rows_hot[i * slots:(i + 1) * slots, pl.ds(start, C)] = jnp.where(
                ids == col_row + i, 1.0, 0.0).astype(jnp.bfloat16)
            rows_hot_t[pl.ds(start, C), i * slots:(i + 1) * slots] = jnp.where(
                ids_t == flat_row + i, 1.0, 0.0).astype(jnp.bfloat16)
        return carry

    lax.fori_loop(0, planes * R // C, one_hot, 0)

    def strided_column(k):
        return pl.ds(column_base + k, 8, columns)

    def rows_at(t):
        return pl.ds(base + t, chunks, tiles)

    def turn(source):
        for t in range(tiles):
            for p in range(planes):
                mixed[t, pl.ds(chunks * p, chunks), :] = source[p, rows_at(t), :]
            turned_in[t, pl.ds(PAD, C), :] = jnp.transpose(mixed[t])

    def turn_back(target):
        for t in range(tiles):
            mixed[t] = jnp.transpose(turned_out[t, pl.ds(PAD, C), :])
            for p in range(planes):
                target[p, rows_at(t), :] = mixed[t, pl.ds(chunks * p, chunks), :]

    def plane_of(at):
        plane = jnp.zeros_like(at)
        for p in range(1, planes):
            plane = jnp.where(at >= chunks * p, p, plane)
        return plane

    for t in range(tiles):
        owner_ref[t] = plane_of(jnp.bitwise_and(lane + (C - chunks * t), C - 1))

    def unfold(landed):
        for h in range(2):
            for t in range(tiles):
                mixed[h, pl.ds(chunks * t, chunks), :] = landed[h, rows_at(t), :]
            folded = jnp.transpose(mixed[h])
            fold_ref[h, pl.ds(8, C), :] = folded
            fold_ref[h, pl.ds(8 + C, 8), :] = folded[:8]
            offset = 8 + w if h else 8 + w - PAD
            for p in range(planes):
                moved_ref[h, p] = pltpu.roll(
                    fold_ref[h, pl.ds(offset + p * w, PAD), :], chunks * p, axis=1)
        for t in range(tiles):
            owner = owner_ref[t]
            mine = [owner == p for p in range(planes)]
            for h in range(2):
                for part in range(0, PAD, 8):
                    block = moved_ref[h, 0, pl.ds(part, 8), :]
                    for p in range(1, planes):
                        block = jnp.where(mine[p], moved_ref[h, p, pl.ds(part, 8), :], block)
                    turned_in[t, pl.ds((PAD + C) * h + part, 8), :] = pltpu.roll(
                        block, (C - chunks * t) % C, axis=1)

    def stencil(source, emit):
        def column(k):
            return [source[t, k] for t in range(tiles)]

        def lean(u, after):
            beyond = after[1:] + [pltpu.roll(after[0], C - 1, axis=1)]
            return [a + b for a, b in zip(u, beyond)]

        here = column(0)
        wrapped = [pltpu.roll(v, 7, axis=0) for v in here]
        slant_end = lean(column(columns - 1), wrapped)
        slant_before = [pltpu.roll(v, 1, axis=0) for v in slant_end]
        for k in range(columns):
            if k < columns - 1:
                after = column(k + 1)
                slant = lean(here, after)
            else:
                slant = slant_end
            below = [pltpu.roll(slant[-1], 1, axis=1)] + slant[:-1]
            for t in range(tiles):
                emit(t, k, here[t], below[t] + slant_before[t])
            here, slant_before = after, slant

    def smooth():
        for t in range(tiles):
            for k in range(columns):
                ping[t, k] = turned_in[t, strided_column(k), :]

        def into(target):
            def emit(t, k, v, near):
                target[t, k] = keep_ref[t, k] * v + gain_ref[t, k] * near
            return emit

        def twice(i, carry):
            stencil(ping, into(pong))
            stencil(pong, into(ping))
            return carry

        lax.fori_loop(0, SWEEPS // 2, twice, 0)
        for t in range(tiles):
            for k in range(columns):
                turned_out[t, strided_column(k), :] = ping[t, k]
        turn_back(smooth_ref)

    def depth_of(rows_of):
        for t in range(tiles):
            mixed[0, pl.ds(chunks * t, chunks), :] = rows_of(rows_at(t)).astype(jnp.float32)
        spare = C - chunks * tiles
        mixed[0, pl.ds(chunks * tiles, spare), :] = jnp.zeros((spare, C), jnp.float32)
        return jnp.transpose(mixed[0]).astype(jnp.bfloat16)

    row_c = lax.broadcasted_iota(jnp.int32, (C, C), 0)
    lane_c = lax.broadcasted_iota(jnp.int32, (C, C), 1)
    chunk_c = lane_c - chunks * plane_of(lane_c)

    def spread_depth(part, emit):
        for t in range(tiles):
            copy_of = jnp.where(row_c == chunk_c + chunks * t, 1.0, 0.0).astype(jnp.bfloat16)
            emit(t, jnp.dot(part, copy_of, preferred_element_type=jnp.float32))

    plane = plane_of(lane)
    lane_level = jnp.where(plane >= levels, plane - levels, plane).astype(jnp.float32)

    def coefficients_main():
        def main(t, value):
            depth_ref[t, pl.ds(PAD, C), :] = value

        spread_depth(depth_of(lambda rows: bottom[rows, :]), main)

    def coefficients():
        def beside(rows):
            east = bottom_side[1, rows, :]
            west = bottom_side[0, rows, :]
            at = lax.broadcasted_iota(jnp.int32, (chunks, C), 1)
            return jnp.where(at < C // 2, east, west)

        def sides(t, value):
            depth_ref[t, pl.ds(0, PAD), :] = value[C - PAD:]
            depth_ref[t, pl.ds(PAD + C, PAD), :] = value[:PAD]

        spread_depth(depth_of(beside), sides)
        for t in range(tiles):
            for k in range(columns):
                pong[t, k] = jnp.where(
                    depth_ref[t, strided_column(k), :] > lane_level, 1.0, 0.0)

        def emit(t, k, wet, near):
            gain = SMOOTHING * wet
            gain_ref[t, k] = gain
            keep_ref[t, k] = wet - gain * near

        stencil(pong, emit)

    def meridional(copies, make, only):
        for i, (dz, dm) in enumerate(copies):
            if (dz == 0) == only:
                when(-dm, lambda i=i: make(i).wait_recv())

    share = pair * half
    give = pltpu.make_async_remote_copy(
        src_ref=back.at[pl.ds((1 - g) * share, share)], dst_ref=back_in,
        send_sem=bg_send, recv_sem=bg_recv, device_id=(1 - g, z, m), device_id_type=MESH)

    def model_step():
        land_all(MERIDIONAL, state_copy)
        for k, dm, row in ((0, -1, 7), (1, 1, 8 + R)):
            def edge_in(k=k, row=row):
                for q in range(fields * half):
                    state[q, pl.ds(row, 1), :] = state_rows_in[k, pl.ds(q, 1), :]
            def edge_none(row=row):
                for q in range(fields * half):
                    state[q, pl.ds(row, 1), :] = jnp.zeros((1, C), jnp.float32)
            pl.when(has[dm])(edge_in)
            pl.when(jnp.logical_not(has[dm]))(edge_none)

        east_bottom = jnp.where(lane_r == C - 1, 0, pltpu.roll(deep, C - 1, axis=1))
        west_bottom = jnp.where(lane_r == 0, 0, pltpu.roll(deep, 1, axis=1))

        def step_level(j, carry):
            level = g * half + j
            wet_c = (deep > level).astype(jnp.float32)
            wet_e = (east_bottom > level).astype(jnp.float32)
            wet_w = (west_bottom > level).astype(jnp.float32)
            wet_n = (bottom[pl.ds(PAD + 1, R), :] > level).astype(jnp.float32)
            wet_s = (bottom[pl.ds(PAD - 1, R), :] > level).astype(jnp.float32)
            vel_x = state[2 * half + j, pl.ds(8, R), :]
            vel_y = state[3 * half + j, pl.ds(8, R), :]
            for f in range(fields):
                q = f * half + j
                centre = state[q, pl.ds(8, R), :]
                east = pltpu.roll(centre, C - 1, axis=1)
                west = pltpu.roll(centre, 1, axis=1)
                north = state[q, pl.ds(9, R), :]
                south = state[q, pl.ds(7, R), :]
                grad_x = 0.5 * (wet_e * east - wet_w * west)
                grad_y = 0.5 * (wet_n * north - wet_s * south)
                flux = wet_c * (
                    wet_e * (east - centre) + wet_w * (west - centre)
                    + wet_n * (north - centre) + wet_s * (south - centre)
                )
                back[q] = wet_c * (
                    centre - ADVECTION * (vel_x * grad_x + vel_y * grad_y) + MIXING * flux
                )
            return carry

        lax.fori_loop(0, half, step_level, 0)
        for k in range(2):
            vel = edge_own[k]
            speed = jnp.zeros((R, C), jnp.float32)
            for f in range(fields):
                speed = jnp.where(
                    lane_r >= f * half, pltpu.roll(vel, (C + (f - 2) * half) % C, axis=1), speed)
            edge_vel[k] = speed

    def edge_step():
        rows = R // fold
        for k in range(2):
            move = C - w - LEDGE if k == 0 else C - LEDGE
            middle = aux_in[3 * k + 1]
            for h in range(fold):
                edge_in[k, pl.ds(h * rows, rows), :] = pltpu.roll(
                    middle, (C - GROUP * h) % C, axis=1)
                bottom_side[k, pl.ds(PAD + h * rows, rows), :] = pltpu.roll(
                    middle, (C + move - GROUP * h) % C, axis=1).astype(jnp.int32)
            for dm, h, start in ((1, fold - 1, 0), (-1, 0, PAD + R)):
                def corner(dm=dm, h=h, start=start, k=k, move=move):
                    bottom_side[k, pl.ds(start, rows), :] = pltpu.roll(
                        aux_in[3 * k + dm + 1], (C + move - GROUP * h) % C, axis=1).astype(jnp.int32)
                when(-dm, corner)
        level_at = lane_r
        for f in range(1, fields):
            level_at = jnp.where(lane_r >= f * half, lane_r - f * half, level_at)
        level_at = (level_at + g * half).astype(jnp.float32)
        corrections = []
        for k in range(2):
            near_lane, own_lane = (LEDGE + w - 1, LEDGE) if k == 0 else (LEDGE, LEDGE + w - 1)
            beyond = edge_in[k]
            own = edge_own[1 - k]
            both = (beyond[:, near_lane:near_lane + 1] > level_at) & (
                own[:, own_lane:own_lane + 1] > level_at)
            drift = (0.5 * ADVECTION if k == 0 else -0.5 * ADVECTION) * edge_vel[1 - k]
            corrections.append(jnp.where(both, (MIXING + drift) * beyond - MIXING * own, 0.0))
        for q in range(fields * half):
            back[q] = back[q] + jnp.where(
                lane_r == 0, pltpu.roll(corrections[0], (C - q) % C, axis=1),
                jnp.where(
                    lane_r == C - 1, pltpu.roll(corrections[1], C - 1 - q, axis=1), 0.0))
        give.start()

    meridional(DIRS, bottom_copy, True)
    model_step()
    coefficients_main()
    meridional(DIRS, one_copy, True)
    turn(field)
    meridional(DIRS, bottom_copy, False)
    edge_step()
    coefficients()
    meridional(DIRS, one_copy, False)
    unfold(strips)
    smooth()
    load_std.wait()
    give.wait_recv()

    def collect(j, carry):
        for f in range(pair):
            for other in range(2):
                if other:
                    p = f * levels + (1 - g) * half + j
                    prior = back_in[f * half + j]
                else:
                    p = f * levels + g * half + j
                    prior = back[(g * pair + f) * half + j]
                rows = pl.ds(pl.multiple_of(p * R, R), R)
                high, low = pieces(std[p] * smooth_ref[p, pl.ds(PAD, R), :] + prior)
                parts_ref[rows, :C] = high
                parts_ref[rows, C:] = low
        return carry

    lax.fori_loop(0, half, collect, 0)
    near_w = corner_hot[0]
    far_w = corner_hot[1]
    picked = jnp.dot(rows_hot[...], parts_ref[...], preferred_element_type=jnp.float32)
    picked = picked[:, :C] + picked[:, C:]
    observed = jnp.sum(picked[:slots] * near_w + picked[slots:] * far_w, axis=1, keepdims=True)
    misfit = scale * (observed - seen)
    spread = jnp.concatenate([near_w * misfit, far_w * misfit], axis=0)
    scattered = jnp.dot(
        rows_hot_t[...], jnp.concatenate(pieces(spread), axis=1), preferred_element_type=jnp.float32)
    x_ref[...] = scattered[:, :C] + scattered[:, C:]

    def weigh(p, carry):
        wet = deep > lax.rem(p, levels)
        adjoint = x_ref[pl.ds(pl.multiple_of(p * R, R), R), :]
        field_two[p, pl.ds(PAD, R), :] = jnp.where(wet, std[p] * adjoint, 0.0)
        return carry

    lax.fori_loop(0, planes, weigh, 0)
    edge = PAD // 8
    outer = [r for r in range(R // 8) if r < edge or r >= R // 8 - edge]
    pack(field_two, strips_out_two, outer)
    for i, (dz, dm) in enumerate(DIRS):
        if dz != 0 and dm != 0:
            when(dm, lambda i=i: two_copy(i).start())
    pack(field_two, strips_out_two, [r for r in range(R // 8) if r not in outer])
    for i, (dz, dm) in enumerate(DIRS):
        if dz == 0 or dm == 0:
            when(dm, lambda i=i: two_copy(i).start())
    meridional(DIRS, two_copy, True)
    turn(field_two)
    meridional(DIRS, two_copy, False)
    unfold(strips_two)
    smooth()

    def write(p, carry):
        out_ref[p] = smooth_ref[p, pl.ds(PAD, R), :]
        return carry

    lax.fori_loop(0, planes, write, 0)
    sent_all(DIRS, bottom_copy)
    sent_all(MERIDIONAL, state_copy)
    sent_all(DIRS, one_copy)
    sent_all(DIRS, two_copy)
    give.wait_send()


def body(
    model_state,
    control,
    error_std,
    bottom_level,
    obs_count,
    obs_corner,
    obs_weight,
    obs_value,
    obs_precision,
    *,
    n_zon,
    n_mer,
):
    fields, half, R, C = model_state.shape
    pair, levels = control.shape[:2]
    planes = pair * levels
    slots = obs_corner.shape[-1]
    ext = R + 2 * PAD
    state_planes = fields * half
    f32 = jnp.float32
    chunks = C // planes
    tiles = (R + 2 * SWEEPS + chunks - 1) // chunks
    turned = pltpu.VMEM((tiles, C + 2 * PAD, C), f32)
    slabs = pltpu.VMEM((tiles, (C + 2 * SWEEPS + 7) // 8, 8, C), f32)
    vmem = pl.BlockSpec(memory_space=pltpu.VMEM)
    hbm = pl.BlockSpec(memory_space=pl.ANY)
    dma = pltpu.SemaphoreType.DMA
    sizes = (n_zon, n_mer, levels, half, pair, fields, R, C)
    row_slots = (state_planes + 7) // 8 * 8
    smoothed = pl.pallas_call(
        functools.partial(kernel, sizes),
        out_shape=pltpu.VMEM((planes, R, C), f32),
        in_specs=[hbm] * 9,
        out_specs=vmem,
        scratch_shapes=[
            pltpu.VMEM((R, C), jnp.int32),
            pltpu.VMEM((1, 1), jnp.int32),
            pltpu.VMEM((1, slots), jnp.int32),
            pltpu.VMEM((4, slots), f32),
            pltpu.VMEM((1, slots), f32),
            pltpu.VMEM((1, slots), f32),
            pltpu.VMEM((state_planes, R + 16, C), f32),
            pltpu.VMEM((2, row_slots, C), f32),
            pltpu.VMEM((2, row_slots, C), f32),
            pltpu.VMEM((2, R, C), f32),
            pltpu.VMEM((2, R, C), f32),
            pltpu.VMEM((2, R, C), f32),
            pltpu.VMEM((2, R * GROUP // C, C), f32),
            pltpu.VMEM((6, R * GROUP // C, C), f32),
            pltpu.VMEM((state_planes, R, C), f32),
            pltpu.VMEM((pair * half, R, C), f32),
            pltpu.VMEM((planes, ext, C), f32),
            pltpu.VMEM((2, R, C), f32),
            pltpu.VMEM((2, ext, C), f32),
            pltpu.VMEM((planes, ext, C), f32),
            pltpu.VMEM((2, R, C), f32),
            pltpu.VMEM((2, ext, C), f32),
            pltpu.VMEM((tiles, C, C), f32),
            turned,
            turned,
            turned,
            pltpu.VMEM((2, C + PAD, C), f32),
            pltpu.VMEM((2, planes, PAD, C), f32),
            pltpu.VMEM((tiles, 8, C), jnp.int32),
            slabs, slabs, slabs, slabs,
            pltpu.VMEM((ext, C), jnp.int32),
            pltpu.VMEM((2, ext, C), jnp.int32),
            pltpu.VMEM((planes, R, C), f32),
            pltpu.VMEM((planes, ext, C), f32),
            pltpu.VMEM((planes * R, C), f32),
            pltpu.VMEM((planes * R, 2 * C), jnp.bfloat16),
            pltpu.VMEM((2 * slots, planes * R), jnp.bfloat16),
            pltpu.VMEM((planes * R, 2 * slots), jnp.bfloat16),
            pltpu.VMEM((128, slots), f32),
            pltpu.VMEM((2, slots, C), f32),
            dma((9,)),
            dma((8,)), dma((8,)),
            dma((2,)), dma((2,)),
            dma((8,)), dma((8,)),
            dma((8,)), dma((8,)),
            dma, dma,
        ],
        compiler_params=pltpu.CompilerParams(collective_id=0, has_side_effects=True),
    )(
        model_state.reshape(state_planes, R, C),
        control.reshape(planes, R, C),
        error_std.reshape(planes, R, C),
        bottom_level,
        obs_count.reshape(1, 1),
        obs_corner.reshape(1, slots),
        obs_weight.reshape(4, slots),
        obs_value.reshape(1, slots),
        obs_precision.reshape(1, slots),
    )
    return control + smoothed.reshape(control.shape)


def solution(mesh):
    return jax.shard_map(
        functools.partial(body, n_zon=mesh.shape["zon"], n_mer=mesh.shape["mer"]),
        mesh=mesh,
        in_specs=(
            P(None, "grp", "mer", "zon"),
            P("grp", None, "mer", "zon"),
            P("grp", None, "mer", "zon"),
            P("mer", "zon"),
            P("grp", "mer", "zon"),
            P("grp", "mer", "zon", None),
            P("grp", "mer", "zon", None, None),
            P("grp", "mer", "zon", None),
            P("grp", "mer", "zon", None),
        ),
        out_specs=P("grp", None, "mer", "zon"),
        check_vma=False,
    )
```
